256 devices in a mesh: ka: 16 (over x, z_hi), row: 16 (over z_lo, y, core).
Axes of the slice: x: 4, y: 4, z: 8 (z_hi: 4, z_lo: 2; z = z_hi * 2 + z_lo), core: 2. Of those that a mesh axis runs over, the one named last changes fastest.
Arguments:
- gauge: bfloat16 [256, 2, 384, 384], P(('ka', 'row')), may hold values from -3 to 3
- energies: float32 [256, 384], P(('ka', 'row')), may hold values from -5 to 5
- kmesh: int32 [3, 256], replicated, may hold values from 0 to 11
- lattice: int32 [3, 1024], P(None, 'row'), may hold values from -8 to 8
- degeneracy: int32 [1024], P('row'), may hold values from 1 to 8
- path: int32 [3, 32], replicated, may hold values from 0 to 63
Outputs:
- lattice_h: bfloat16 [1024, 384, 768], P('row', 'ka')
- path_h: float32 [32, 384, 768], P('row', 'ka')
The draws below stay inside these ranges and needn't reach their ends.
All inputs are finite; a program needn't handle non-finite values.
Results may differ from the reference program's by a relative error of at most 0.006.
Values may be sent and summed in bfloat16 or wider, within the bound.
A program may use at most 64 MiB of HBM per device.

```python
import math
import jax
import jax.numpy as jnp
from jax import lax

W = 384
MESH = 12
PATH_DEN = 64
R_DEV = 64
NK = 256
NR = 1024
NP = 32
N_ROW = 16


def plant(result, rng, least, top_value):
    index_at = [jax.random.randint(jax.random.fold_in(rng, axis), (), 0, length) for axis, length in enumerate(result.shape)]
    widest = result.shape.index(max(result.shape))
    beside = index_at[:widest] + [(index_at[widest] + 1) % result.shape[widest]] + index_at[widest + 1:]
    return result.at[tuple(index_at)].set(least).at[tuple(beside)].set(top_value)


def block_levels(rng, extent, split, low, high):
    def one(position, shards_of):
        steps = jax.random.uniform(jax.random.fold_in(jax.random.fold_in(rng, 6), position), (shards_of,), jnp.float32, low / len(split), high / len(split))
        return jnp.repeat(jnp.exp(steps), extent[position] // shards_of).reshape((-1,) + (1,) * (len(extent) - position - 1))

    loudness = one(*split[0])
    for cut in split[1:]:
        loudness = loudness * one(*cut)
    return loudness


def bell_draw(own_key, shape, deviation, reach, pieces=(), held_as=jnp.bfloat16):
    array = jax.random.normal(own_key, shape, jnp.float32) * deviation
    if len(pieces) > 0:
        array = block_levels(own_key, shape, pieces, -0.22, 0.18) * array
    return jnp.clip(array, min=-reach, max=reach).astype(held_as)


def setup_inputs(seed: int = 0) -> dict:
    arg_keys = jax.random.split(jax.random.key(seed), 7)
    return {
        "gauge": bell_draw(arg_keys[0], (NK, 2, W, W), 0.5, 3.0, ((0, 256),)),
        "energies": bell_draw(arg_keys[1], (NK, W), 1.0, 5.0, ((0, 256),), jnp.float32),
        "kmesh": plant(jax.random.randint(arg_keys[2], (3, NK), 0, MESH), jax.random.fold_in(arg_keys[2], 1), 0, MESH - 1).astype(jnp.int32),
        "lattice": plant(jax.random.randint(arg_keys[3], (3, NR), -8, 9), jax.random.fold_in(arg_keys[3], 1), -8, 8).astype(jnp.int32),
        "degeneracy": plant(jax.random.randint(arg_keys[4], (NR,), 1, 9), jax.random.fold_in(arg_keys[4], 1), 1, 8).astype(jnp.int32),
        "path": plant(jax.random.randint(arg_keys[5], (3, NP), 0, PATH_DEN), jax.random.fold_in(arg_keys[5], 1), 0, PATH_DEN - 1).astype(jnp.int32),
    }


def rotate(pair):
    gauge_one, energy_one = pair
    scaled = (energy_one[None, :, None] * gauge_one.astype(jnp.float32)).astype(jnp.bfloat16)
    scaled_re = scaled[0].astype(jnp.float32)
    scaled_im = scaled[1].astype(jnp.float32)
    stacked = jnp.concatenate([gauge_one[0], gauge_one[1]], 0).astype(jnp.float32)
    partner = jnp.concatenate([jnp.concatenate([scaled_re, scaled_im], 1), jnp.concatenate([scaled_im, -scaled_re], 1)], 0)
    return jnp.dot(stacked.T, partner, preferred_element_type=jnp.float32).astype(jnp.bfloat16)


def reference(gauge, energies, kmesh, lattice, degeneracy, path):
    k_total = kmesh.shape[1]
    orbitals = gauge.shape[2]
    path_total = path.shape[1]
    rotated = lax.map(rotate, (gauge, energies))
    flattened = rotated.reshape(k_total, -1).astype(jnp.float32)
    vector_blocks = lattice.reshape(3, N_ROW, R_DEV).transpose(1, 0, 2)
    multiples = degeneracy.reshape(N_ROW, R_DEV)

    def step_block(running, block_in):
        vectors, counts_r = block_in
        windings = jnp.mod(jnp.sum(vectors[:, :, None] * kmesh[:, None, :], 0), MESH).astype(jnp.int32)
        angles = windings.astype(jnp.float32) * (2.0 * math.pi / MESH)
        factors = jnp.concatenate([jnp.cos(angles), jnp.sin(angles)], 0).astype(jnp.bfloat16)
        factors = lax.optimization_barrier(factors).astype(jnp.float32)
        products = jnp.dot(factors, flattened, preferred_element_type=jnp.float32)
        products = products.reshape(2, R_DEV, orbitals, 2, orbitals)
        real_part = products[0, :, :, 0] + products[1, :, :, 1]
        imag_part = products[0, :, :, 1] - products[1, :, :, 0]
        lattice_f = jnp.concatenate([real_part, imag_part], -1) / k_total
        windings_p = jnp.mod(jnp.sum(path[:, :, None] * vectors[:, None, :], 0), PATH_DEN).astype(jnp.int32)
        angles_p = windings_p.astype(jnp.float32) * (2.0 * math.pi / PATH_DEN)
        weights = 1.0 / counts_r.astype(jnp.float32)
        factors_p = jnp.concatenate([jnp.cos(angles_p) * weights[None, :], jnp.sin(angles_p) * weights[None, :]], 0).astype(jnp.bfloat16)
        factors_p = lax.optimization_barrier(factors_p).astype(jnp.float32)
        values = jnp.dot(factors_p, lattice_f.reshape(R_DEV, -1), preferred_element_type=jnp.float32)
        values = values.reshape(2, path_total, orbitals, 2, orbitals)
        real_p = values[0, :, :, 0] - values[1, :, :, 1]
        imag_p = values[0, :, :, 1] + values[1, :, :, 0]
        return running + jnp.concatenate([real_p, imag_p], -1), lattice_f.astype(jnp.bfloat16)

    initial = jnp.zeros((path_total, orbitals, 2 * orbitals), jnp.float32)
    path_h, blocks = lax.scan(step_block, initial, (vector_blocks, multiples))
    lattice_h = blocks.reshape(N_ROW * R_DEV, orbitals, 2 * orbitals)
    return lattice_h, path_h
```

```python
import functools
import math

import jax
import jax.numpy as jnp
from jax import lax
from jax.experimental import pallas as pl
from jax.experimental.pallas import tpu as pltpu
from jax.sharding import PartitionSpec as P

MESH = 12
PATH_DEN = 64
NKA = 16
NROW = 16
ROWS = 24
TILES = 3
PARTS = 2
HALF = ROWS // 2
SUB = HALF // PARTS
CHUNKS = TILES * PARTS
UNIT = 2 * SUB
Y_FIRST = ()

BF = jnp.bfloat16
F32 = jnp.float32


def kernel(
    gauge, energies, kmesh, lattice, degeneracy, path,
    out_l, out_p,
    at_ref, sc_ref, send, arrived, plain, other, gath, lmat, fpart, mixp, mixr,
    stage_l, stage_p,
    a2a_s, a2a_r, g_s, g_r, f_s, f_r, m_s, m_r, o_s, o_r, op_s, op_r,
):
    ka = lax.axis_index("ka")
    row = lax.axis_index("row")
    core = row % 2
    y = (row // 2) % 4
    zlo = row // 8
    mate = row + 1 - 2 * core

    def unit_of(z, yy, c):
        return z * 8 + yy * 2 + c

    yp = (y + 1) % 4
    ym = (y + 3) % 4
    yo = (y + 2) % 4
    zo = 1 - zlo

    barrier = pltpu.get_barrier_semaphore()
    for i in range(1, NKA):
        pl.semaphore_signal(
            barrier, inc=1, device_id=((ka + i) % NKA, row), device_id_type=pl.DeviceIdType.MESH
        )
    for i in range(1, NROW):
        pl.semaphore_signal(
            barrier, inc=1, device_id=(ka, (row + i) % NROW), device_id_type=pl.DeviceIdType.MESH
        )

    def remote(src, dst, ssem, rsem, dev):
        return pltpu.make_async_remote_copy(
            src_ref=src, dst_ref=dst, send_sem=ssem, recv_sem=rsem,
            device_id=dev, device_id_type=pl.DeviceIdType.MESH,
        )

    def wait_bytes(ref, sem):
        pltpu.make_async_copy(ref, ref, sem).wait()

    w = gauge.shape[1]
    e_col = jnp.transpose(jnp.broadcast_to(energies[...], (128, w)))
    e_full = jnp.concatenate([e_col] * (w // 128), 1)
    for p in range(2):
        u = gauge[p].astype(F32)
        at_ref[:, p * w : (p + 1) * w] = jnp.transpose(u).astype(BF)
        sc_ref[p] = (e_full * u).astype(BF)

    def rotate(cc):
        cols = slice(cc * 128, cc * 128 + 128)
        sr = sc_ref[0, :, cols]
        si = sc_ref[1, :, cols]
        rhs = jnp.concatenate(
            [jnp.concatenate([sr, si], 1), jnp.concatenate([si, -sr], 1)], 0
        )
        h = jnp.dot(at_ref[...], rhs, preferred_element_type=F32)
        for j in range(NKA):
            both = jnp.concatenate(
                [h[j * ROWS : (j + 1) * ROWS, :128], h[j * ROWS : (j + 1) * ROWS, 128:]], 0
            )
            send[cc, j] = both.astype(BF)

    def spread(cc):
        for i in range(1, NKA):
            j = (ka + i) % NKA
            remote(send.at[cc, j], arrived.at[cc, ka], a2a_s.at[cc], a2a_r.at[cc], (j, row)).start()
        arrived[cc, pl.ds(ka, 1)] = send[cc, pl.ds(ka, 1)]

    rotate(0)
    pl.semaphore_wait(barrier, NKA - 1 + NROW - 1)
    spread(0)
    rotate(1)
    spread(1)
    rotate(2)

    nk = kmesh.shape[1]
    r_dev = lattice.shape[1]
    np_all = path.shape[1]

    def pad_rows(a):
        return jnp.concatenate([a.astype(F32), jnp.zeros((13, a.shape[1]), F32)], 0).astype(BF)

    lat = pad_rows(lattice[...])
    at_k = lax.broadcasted_iota(jnp.int32, (nk, nk), 0)
    to_k = lax.broadcasted_iota(jnp.int32, (nk, nk), 1)
    order = jnp.where(at_k == (to_k % NROW) * NROW + to_k // NKA, 1.0, 0.0).astype(BF)
    km = jnp.dot(pad_rows(kmesh[...]), order, preferred_element_type=F32).astype(BF)
    dims = (((0,), (0,)), ((), ()))
    wind = lax.dot_general(lat, km, dims, preferred_element_type=F32).astype(jnp.int32)
    wind = jnp.mod(wind + 23 * MESH, MESH)
    angle = wind.astype(F32) * (2.0 * math.pi / MESH)
    fcos = jnp.cos(angle).astype(BF)
    fsin = jnp.sin(angle).astype(BF)
    fpart[0, :, :nk] = fcos
    fpart[0, :, nk:] = fsin
    f_copy = remote(fpart.at[0], fpart.at[1], f_s, f_r, (ka, mate))
    f_copy.start()
    wind_p = lax.dot_general(pad_rows(path[...]), lat, dims, preferred_element_type=F32)
    wind_p = jnp.mod(wind_p.astype(jnp.int32) + 24 * PATH_DEN, PATH_DEN)
    angle_p = wind_p.astype(F32) * (2.0 * math.pi / PATH_DEN)
    weights = 1.0 / degeneracy[...].astype(F32)
    pcos = (jnp.cos(angle_p) * weights).astype(BF)
    psin = (jnp.sin(angle_p) * weights).astype(BF)
    pboth = jnp.concatenate([pcos, psin], 0)
    mc = jnp.dot(pboth, fcos, preferred_element_type=F32)
    ms = jnp.dot(pboth, fsin, preferred_element_type=F32)
    m_re = mc[:np_all] + ms[np_all:]
    m_im = mc[np_all:] - ms[:np_all]
    per_chip = np_all // (NROW // 2)
    for p in range(NROW // 2):
        mixp[p, :per_chip] = m_re[p * per_chip : (p + 1) * per_chip]
        mixp[p, per_chip:] = m_im[p * per_chip : (p + 1) * per_chip]
    for i in range(1, NROW):
        to = (row + i) % NROW
        remote(mixp.at[to // 2], mixr.at[row], m_s, m_r, (ka, to)).start()
    mixr[pl.ds(row, 1)] = mixp[pl.ds(row // 2, 1)]

    def transpose(cc):
        wait_bytes(arrived.at[cc, pl.ds(0, NKA - 1)], a2a_r.at[cc])
        plain[...] = arrived[cc].reshape(NKA * 2 * ROWS, 128).astype(F32)
        for part in range(PARTS):
            g = cc * PARTS + part
            for p in range(2):
                for a in range(SUB):
                    at = p * ROWS + part * SUB + a
                    mine = plain[pl.ds(at + core * HALF, NKA, stride=2 * ROWS), :]
                    gath[g, row, p * SUB + a] = mine.astype(BF)
                    his = plain[pl.ds(at + (1 - core) * HALF, NKA, stride=2 * ROWS), :]
                    other[g, p * SUB + a] = his.astype(BF)
            remote(other.at[g], gath.at[g, row], g_s.at[g], g_r.at[g, row], (ka, mate)).start()
            scatter(g, row)

    def pass_on(g, u, to):
        remote(gath.at[g, u], gath.at[g, u], g_s.at[g], g_r.at[g, u], (ka, to)).start()

    def landed(g, u):
        wait_bytes(gath.at[g, u], g_r.at[g, u])

    def scatter(g, u):
        pass_on(g, u, unit_of(zlo, yp, core))
        pass_on(g, u, unit_of(zlo, ym, core))
        if g not in Y_FIRST:
            pass_on(g, u, unit_of(zo, y, core))

    def from_mate(g):
        landed(g, mate)
        scatter(g, mate)

    def relay(g, z):
        for c in range(2):
            um = unit_of(z, ym, c)
            landed(g, um)
            if c == 0:
                pass_on(g, um, unit_of(zlo, yp, core))
            if g in Y_FIRST:
                pass_on(g, um, unit_of(zo, y, core))
            up = unit_of(z, yp, c)
            landed(g, up)
            if c == 1:
                pass_on(g, up, unit_of(zlo, ym, core))
            if g in Y_FIRST:
                pass_on(g, up, unit_of(zo, y, core))

    def y_far(g, z):
        for c in range(2):
            u = unit_of(z, yo, c)
            landed(g, u)
            if g in Y_FIRST:
                pass_on(g, u, unit_of(zo, y, core))

    def own_plane(g):
        relay(g, zlo)
        if g in Y_FIRST:
            for c in range(2):
                u = unit_of(zlo, y, c)
                pass_on(g, u, unit_of(zo, y, core))
            y_far(g, zlo)

    def z_arrivals(g):
        if g in Y_FIRST:
            return
        for c in range(2):
            u = unit_of(zo, y, c)
            landed(g, u)
            pass_on(g, u, unit_of(zlo, yp, core))
            pass_on(g, u, unit_of(zlo, ym, core))

    def other_plane(g):
        if g not in Y_FIRST:
            relay(g, zo)

    def last_units(g):
        if g in Y_FIRST:
            for yy in range(4):
                for c in range(2):
                    landed(g, unit_of(zo, yy, c))
        else:
            y_far(g, zlo)
            y_far(g, zo)

    def build_factors():
        wait_bytes(mixr.at[pl.ds(0, NROW - 1)], m_r)
        f_copy.wait()
        for s in range(2):
            at = s * 2 * r_dev
            c_part = fpart[s, :, :nk]
            s_part = fpart[s, :, nk:]
            lmat[at : at + r_dev, :nk] = c_part
            lmat[at : at + r_dev, nk:] = s_part
            lmat[at + r_dev : at + 2 * r_dev, :nk] = -s_part
            lmat[at + r_dev : at + 2 * r_dev, nk:] = c_part
        total = mixr[0]
        for i in range(1, NROW):
            total = total + mixr[i]
        m_r4 = total[:per_chip]
        m_i4 = total[per_chip:]
        wide = jnp.concatenate(
            [jnp.concatenate([m_r4, -m_i4], 1), jnp.concatenate([m_i4, m_r4], 1)], 0
        )
        high = wide.astype(BF)
        low = (wide - high.astype(F32)).astype(BF)
        lmat[4 * r_dev :, :] = jnp.concatenate([high.astype(F32), low.astype(F32)], 0).astype(BF)

    scale = 1.0 / nk

    def transform(g):
        last_units(g)

        def one(i, carry):
            a = 2 * i
            re0 = gath[g, :, a].reshape(nk, 128)
            re1 = gath[g, :, a + 1].reshape(nk, 128)
            im0 = gath[g, :, SUB + a].reshape(nk, 128)
            im1 = gath[g, :, SUB + a + 1].reshape(nk, 128)
            x = jnp.concatenate(
                [jnp.concatenate([re0, re1], 1), jnp.concatenate([im0, im1], 1)], 0
            )
            y_all = jnp.dot(lmat[...], x, preferred_element_type=F32) * scale
            for b in range(2):
                v = y_all[:, b * 128 : b * 128 + 128]
                for p in range(2):
                    out_l[core, g, p, a + b] = v[p * r_dev : (p + 1) * r_dev].astype(BF)
                    stage_l[g, p, a + b] = v[(2 + p) * r_dev : (3 + p) * r_dev].astype(BF)
                vp = v[4 * r_dev : 4 * r_dev + 8] + v[4 * r_dev + 8 :]
                out_p[core, g, a + b] = vp
                stage_p[g, a + b] = vp
            return carry

        lax.fori_loop(0, SUB // 2, one, 0)
        remote(stage_l.at[g], out_l.at[core, g], o_s.at[g], o_r.at[g], (ka, mate)).start()
        remote(stage_p.at[g], out_p.at[core, g], op_s.at[g], op_r.at[g], (ka, mate)).start()

    transpose(0)
    from_mate(0)
    from_mate(1)
    spread(2)
    own_plane(0)
    own_plane(1)
    transpose(1)
    from_mate(2)
    from_mate(3)
    z_arrivals(0)
    z_arrivals(1)
    other_plane(0)
    other_plane(1)
    transpose(2)
    from_mate(4)
    from_mate(5)
    own_plane(2)
    own_plane(3)
    build_factors()
    z_arrivals(2)
    z_arrivals(3)
    transform(0)
    transform(1)
    other_plane(2)
    other_plane(3)
    own_plane(4)
    own_plane(5)
    z_arrivals(4)
    z_arrivals(5)
    transform(2)
    transform(3)
    other_plane(4)
    other_plane(5)
    transform(4)
    transform(5)

    for cc in range(TILES):
        wait_bytes(send.at[cc, pl.ds(0, NKA - 1)], a2a_s.at[cc])
    wait_bytes(mixr.at[pl.ds(0, NROW - 1)], m_s)
    for g in range(CHUNKS):
        wait_bytes(gath.at[g, pl.ds(0, NROW - 1)], g_s.at[g])
        wait_bytes(stage_l.at[g], o_s.at[g])
        wait_bytes(stage_p.at[g], op_s.at[g])
        wait_bytes(stage_l.at[g], o_r.at[g])
        wait_bytes(stage_p.at[g], op_r.at[g])


def local(gauge, energies, kmesh, lattice, degeneracy, path):
    w = gauge.shape[2]
    nk = kmesh.shape[1]
    r_dev = lattice.shape[1]
    path_dev = path.shape[1] // NROW
    vmem = pl.BlockSpec(memory_space=pltpu.VMEM)
    dma = pltpu.SemaphoreType.DMA
    out_l, out_p = pl.pallas_call(
        kernel,
        out_shape=(
            jax.ShapeDtypeStruct((2, CHUNKS, 2, SUB, r_dev, 128), BF),
            jax.ShapeDtypeStruct((2, CHUNKS, SUB, 8, 128), F32),
        ),
        in_specs=[vmem] * 6,
        out_specs=(vmem, vmem),
        scratch_shapes=[
            pltpu.VMEM((w, 2 * w), BF),
            pltpu.VMEM((2, w, w), BF),
            pltpu.VMEM((TILES, NKA, 2 * ROWS, 128), BF),
            pltpu.VMEM((TILES, NKA, 2 * ROWS, 128), BF),
            pltpu.VMEM((NKA * 2 * ROWS, 128), F32),
            pltpu.VMEM((CHUNKS, UNIT, NKA, 128), BF),
            pltpu.VMEM((CHUNKS, NROW, UNIT, NKA, 128), BF),
            pltpu.VMEM((4 * r_dev + 16, 2 * nk), BF),
            pltpu.VMEM((2, r_dev, 2 * nk), BF),
            pltpu.VMEM((NROW // 2, 8, nk), F32),
            pltpu.VMEM((NROW, 8, nk), F32),
            pltpu.VMEM((CHUNKS, 2, SUB, r_dev, 128), BF),
            pltpu.VMEM((CHUNKS, SUB, 8, 128), F32),
            dma((TILES,)),
            dma((TILES,)),
            dma((CHUNKS,)),
            dma((CHUNKS, NROW)),
            dma,
            dma,
            dma,
            dma,
            dma((CHUNKS,)),
            dma((CHUNKS,)),
            dma((CHUNKS,)),
            dma((CHUNKS,)),
        ],
        compiler_params=pltpu.CompilerParams(
            collective_id=0, has_side_effects=True, vmem_limit_bytes=40 << 20
        ),
    )(gauge[0], energies, kmesh, lattice, degeneracy[None, :], path)
    lat = out_l.reshape(2, TILES, PARTS, 2, SUB, r_dev, 128)
    lattice_h = lat.transpose(5, 0, 2, 4, 3, 1, 6).reshape(r_dev, ROWS, 2 * w)
    core = lax.axis_index("row") % 2
    pth = out_p.reshape(2, TILES, PARTS, SUB, 2, 2, path_dev, 128)
    pth = lax.dynamic_index_in_dim(pth, core, 5, keepdims=False)
    path_h = pth.transpose(5, 0, 2, 3, 4, 1, 6).reshape(path_dev, ROWS, 2 * w)
    return lattice_h, path_h


def solution(mesh):
    return jax.shard_map(
        local,
        mesh=mesh,
        in_specs=(
            P(("ka", "row"), None, None, None),
            P(("ka", "row"), None),
            P(),
            P(None, "row"),
            P("row"),
            P(),
        ),
        out_specs=(P("row", "ka", None), P("row", "ka", None)),
        check_vma=False,
    )
```

```python
import functools
import math

import jax
import jax.numpy as jnp
from jax import lax
from jax.experimental import pallas as pl
from jax.experimental.pallas import tpu as pltpu
from jax.sharding import PartitionSpec as P

MESH = 12
PATH_DEN = 64
NKA = 16
NROW = 16
ROWS = 24
TILES = 3
PARTS = 2
HALF = ROWS // 2
SUB = HALF // PARTS
CHUNKS = TILES * PARTS
UNIT = 2 * SUB
Y_FIRST = (3,)

BF = jnp.bfloat16
F32 = jnp.float32


def kernel(
    gauge_h, energies_h, kmesh_h, lattice_h, degeneracy_h, path_h,
    out_l, out_p,
    gauge, energies, kmesh, lattice, degeneracy, path, in_s,
    at_ref, sc_ref, send, arrived, plain, other, gath, lmat, fpart, mixp, mixr,
    stage_l, stage_p, from_l, from_p, rows_f, rows_p, mix_f,
    a2a_s, a2a_r, g_s, g_r, f_s, f_r, m_s, m_r, o_s, o_r, op_s, op_r,
):
    loads = [
        pltpu.make_async_copy(src, dst, in_s.at[i])
        for i, (src, dst) in enumerate(
            (
                (energies_h, energies), (gauge_h, gauge), (kmesh_h, kmesh),
                (lattice_h, lattice), (degeneracy_h, degeneracy), (path_h, path),
            )
        )
    ]
    for load in loads:
        load.start()

    ka = lax.axis_index("ka")
    row = lax.axis_index("row")
    core = row % 2
    y = (row // 2) % 4
    zlo = row // 8
    x = ka // 4
    z = (ka % 4) * 2 + zlo
    turn = 2 * zlo - 1
    peers = [(dx, d) for d in (3, 2, 1, 0) for dx in (2, 1, 3, 0) if dx or d]

    def place_of(xx, zz):
        return (xx % 4) * 4 + zz // 2, (zz % 2) * 8 + row % 8
    mate = row + 1 - 2 * core

    def unit_of(z, yy, c):
        return z * 8 + yy * 2 + c

    yp = (y + 1) % 4
    ym = (y + 3) % 4
    yo = (y + 2) % 4
    zo = 1 - zlo

    barrier = pltpu.get_barrier_semaphore()
    for dx, d in peers:
        pl.semaphore_signal(
            barrier, inc=1, device_id=place_of(x + dx, (z + turn * d + 8) % 8),
            device_id_type=pl.DeviceIdType.MESH,
        )
    for i in range(1, NROW):
        pl.semaphore_signal(
            barrier, inc=1, device_id=(ka, (row + i) % NROW), device_id_type=pl.DeviceIdType.MESH
        )

    def remote(src, dst, ssem, rsem, dev):
        return pltpu.make_async_remote_copy(
            src_ref=src, dst_ref=dst, send_sem=ssem, recv_sem=rsem,
            device_id=dev, device_id_type=pl.DeviceIdType.MESH,
        )

    def wait_bytes(ref, sem):
        pltpu.make_async_copy(ref, ref, sem).wait()

    loads[0].wait()
    loads[1].wait()
    w = gauge.shape[1]
    e_col = jnp.transpose(jnp.broadcast_to(energies[...], (128, w)))
    e_full = jnp.concatenate([e_col] * (w // 128), 1)
    for p in range(2):
        u = gauge[p].astype(F32)
        at_ref[:, p * w : (p + 1) * w] = jnp.transpose(u).astype(BF)
        sc_ref[p] = (e_full * u).astype(BF)

    def rotate(cc):
        cols = slice(cc * 128, cc * 128 + 128)
        sr = sc_ref[0, :, cols]
        si = sc_ref[1, :, cols]
        rhs = jnp.concatenate(
            [jnp.concatenate([sr, si], 1), jnp.concatenate([si, -sr], 1)], 0
        )
        h = jnp.dot(at_ref[...], rhs, preferred_element_type=F32)
        for j in range(NKA):
            both = jnp.concatenate(
                [h[j * ROWS : (j + 1) * ROWS, :128], h[j * ROWS : (j + 1) * ROWS, 128:]], 0
            )
            send[cc, j] = both.astype(BF)

    def spread(cc):
        for dx, d in peers:
            to = place_of(x + dx, (z + turn * (0, 1, -2, 3)[d] + 8) % 8)
            remote(
                send.at[cc, to[0]], arrived.at[cc, x * 4 + d], a2a_s.at[cc], a2a_r.at[cc], to
            ).start()
        arrived[cc, pl.ds(x * 4, 1)] = send[cc, pl.ds(ka, 1)]

    rotate(0)
    pl.semaphore_wait(barrier, NKA - 1 + NROW - 1)
    spread(0)
    rotate(1)
    spread(1)
    rotate(2)

    for load in loads[2:]:
        load.wait()
    nk = kmesh.shape[1]
    r_dev = lattice.shape[1]
    np_all = path.shape[1]

    def pad_rows(a):
        return jnp.concatenate([a.astype(F32), jnp.zeros((13, a.shape[1]), F32)], 0).astype(BF)

    lat = pad_rows(lattice[...])
    at_k = lax.broadcasted_iota(jnp.int32, (nk, nk), 0)
    pos = lax.broadcasted_iota(jnp.int32, (8, nk), 1)
    pos_z = pos >> 7
    from_z = ((ka % 4) * 2 + pos_z + (2 * pos_z - 1) * (pos & 3) + 8) & 7
    source = ((((pos >> 2) & 3) * 4 + (from_z >> 1)) * NROW) + (from_z & 1) * 8 + ((pos >> 4) & 7)
    order = jnp.where(at_k == source[:1], 1.0, 0.0).astype(BF)
    km = jnp.dot(pad_rows(kmesh[...]), order, preferred_element_type=F32).astype(BF)
    dims = (((0,), (0,)), ((), ()))
    wind = lax.dot_general(lat, km, dims, preferred_element_type=F32).astype(jnp.int32)
    wind = jnp.mod(wind + 23 * MESH, MESH)
    angle = wind.astype(F32) * (2.0 * math.pi / MESH)
    fcos = jnp.cos(angle).astype(BF)
    fsin = jnp.sin(angle).astype(BF)
    fpart[0, :, :nk] = fcos
    fpart[0, :, nk:] = fsin
    f_copy = remote(fpart.at[0], fpart.at[1], f_s, f_r, (ka, mate))
    f_copy.start()
    wind_p = lax.dot_general(pad_rows(path[...]), lat, dims, preferred_element_type=F32)
    wind_p = jnp.mod(wind_p.astype(jnp.int32) + 24 * PATH_DEN, PATH_DEN)
    angle_p = wind_p.astype(F32) * (2.0 * math.pi / PATH_DEN)
    weights = 1.0 / degeneracy[...].astype(F32)
    pcos = (jnp.cos(angle_p) * weights).astype(BF)
    psin = (jnp.sin(angle_p) * weights).astype(BF)
    pboth = jnp.concatenate([pcos, psin], 0)
    mc = jnp.dot(pboth, fcos, preferred_element_type=F32)
    ms = jnp.dot(pboth, fsin, preferred_element_type=F32)
    m_re = mc[:np_all] + ms[np_all:]
    m_im = mc[np_all:] - ms[:np_all]
    per_chip = np_all // (NROW // 2)
    for p in range(NROW // 2):
        mixp[p, :per_chip] = m_re[p * per_chip : (p + 1) * per_chip]
        mixp[p, per_chip:] = m_im[p * per_chip : (p + 1) * per_chip]
    for i in range(1, NROW):
        to = (row + i) % NROW
        remote(mixp.at[to // 2], mixr.at[row], m_s, m_r, (ka, to)).start()
    mixr[pl.ds(row, 1)] = mixp[pl.ds(row // 2, 1)]

    def transpose(cc):
        wait_bytes(arrived.at[cc, pl.ds(0, NKA - 1)], a2a_r.at[cc])
        plain[...] = arrived[cc].reshape(NKA * 2 * ROWS, 128).astype(F32)
        for part in range(PARTS):
            g = cc * PARTS + part
            for p in range(2):
                for a in range(SUB):
                    at = p * ROWS + part * SUB + a
                    mine = plain[pl.ds(at + core * HALF, NKA, stride=2 * ROWS), :]
                    gath[g, row, p * SUB + a] = mine.astype(BF)
                    his = plain[pl.ds(at + (1 - core) * HALF, NKA, stride=2 * ROWS), :]
                    other[g, p * SUB + a] = his.astype(BF)
            remote(other.at[g], gath.at[g, row], g_s.at[g], g_r.at[g, row], (ka, mate)).start()
            scatter(g, row)

    def pass_on(g, u, to):
        remote(gath.at[g, u], gath.at[g, u], g_s.at[g], g_r.at[g, u], (ka, to)).start()

    def landed(g, u):
        wait_bytes(gath.at[g, u], g_r.at[g, u])

    def scatter(g, u):
        pass_on(g, u, unit_of(zlo, yp, core))
        pass_on(g, u, unit_of(zlo, ym, core))
        if g not in Y_FIRST:
            pass_on(g, u, unit_of(zo, y, core))

    def from_mate(g):
        landed(g, mate)
        scatter(g, mate)

    def relay(g, z):
        for c in range(2):
            um = unit_of(z, ym, c)
            landed(g, um)
            if c == 0:
                pass_on(g, um, unit_of(zlo, yp, core))
            if g in Y_FIRST:
                pass_on(g, um, unit_of(zo, y, core))
            up = unit_of(z, yp, c)
            landed(g, up)
            if c == 1:
                pass_on(g, up, unit_of(zlo, ym, core))
            if g in Y_FIRST:
                pass_on(g, up, unit_of(zo, y, core))

    def y_far(g, z):
        for c in range(2):
            u = unit_of(z, yo, c)
            landed(g, u)
            if g in Y_FIRST:
                pass_on(g, u, unit_of(zo, y, core))

    def own_plane(g):
        relay(g, zlo)
        if g in Y_FIRST:
            for c in range(2):
                u = unit_of(zlo, y, c)
                pass_on(g, u, unit_of(zo, y, core))
            y_far(g, zlo)

    def z_arrivals(g):
        if g in Y_FIRST:
            return
        for c in range(2):
            u = unit_of(zo, y, c)
            landed(g, u)
            pass_on(g, u, unit_of(zlo, yp, core))
            pass_on(g, u, unit_of(zlo, ym, core))

    def other_plane(g):
        if g not in Y_FIRST:
            relay(g, zo)

    def last_units(g):
        if g in Y_FIRST:
            for yy in range(4):
                for c in range(2):
                    landed(g, unit_of(zo, yy, c))
        else:
            y_far(g, zlo)
            y_far(g, zo)

    def build_factors():
        wait_bytes(mixr.at[pl.ds(0, NROW - 1)], m_r)
        f_copy.wait()
        for s in range(2):
            at = s * 2 * r_dev
            c_part = fpart[s, :, :nk]
            s_part = fpart[s, :, nk:]
            lmat[at : at + r_dev, :nk] = c_part
            lmat[at : at + r_dev, nk:] = s_part
            lmat[at + r_dev : at + 2 * r_dev, :nk] = -s_part
            lmat[at + r_dev : at + 2 * r_dev, nk:] = c_part
        total = mixr[0]
        for i in range(1, NROW):
            total = total + mixr[i]
        m_r4 = total[:per_chip]
        m_i4 = total[per_chip:]
        wide = jnp.concatenate(
            [jnp.concatenate([m_r4, -m_i4], 1), jnp.concatenate([m_i4, m_r4], 1)], 0
        )
        own_q = per_chip // 2
        for i in range(4):
            mix_f[i] = wide[i * own_q : (i + 1) * own_q]
        wide = jnp.concatenate([mix_f[2 * p + c] for c in (core, 1 - core) for p in range(2)], 0)
        high = wide.astype(BF)
        low = (wide - high.astype(F32)).astype(BF)
        lmat[4 * r_dev :, :] = jnp.concatenate([high.astype(F32), low.astype(F32)], 0).astype(BF)

    scale = 1.0 / nk

    def transform(g):
        last_units(g)
        cc = g // PARTS
        first = (g % PARTS) * SUB

        def one(i, carry):
            a = 2 * i
            re0 = gath[g, :, a].reshape(nk, 128)
            re1 = gath[g, :, a + 1].reshape(nk, 128)
            im0 = gath[g, :, SUB + a].reshape(nk, 128)
            im1 = gath[g, :, SUB + a + 1].reshape(nk, 128)
            x = jnp.concatenate(
                [jnp.concatenate([re0, re1], 1), jnp.concatenate([im0, im1], 1)], 0
            )
            y_all = jnp.dot(lmat[...], x, preferred_element_type=F32) * scale
            for b in range(2):
                v = y_all[:, b * 128 : b * 128 + 128]
                for p in range(2):
                    place(cc, p, core * HALF + first + a + b, v[p * r_dev : (p + 1) * r_dev])
                    stage_l[g, p, a + b] = v[(2 + p) * r_dev : (3 + p) * r_dev].astype(BF)
                vp = v[4 * r_dev : 4 * r_dev + 8] + v[4 * r_dev + 8 :]
                place_path(cc, core * HALF + first + a + b, vp[:4])
                stage_p[g, a + b] = vp
            return carry

        lax.fori_loop(0, SUB // 2, one, 0)
        remote(stage_l.at[g], from_l.at[g], o_s.at[g], o_r.at[g], (ka, mate)).start()
        remote(stage_p.at[g], from_p.at[g], op_s.at[g], op_r.at[g], (ka, mate)).start()

    def place(cc, p, a, value):
        rows_f[cc, p, pl.ds(a, r_dev, stride=ROWS), :] = value

    def place_path(cc, a, value):
        for p in range(2):
            rows_p[cc, p, pl.ds(a, 2, stride=ROWS), :] = value[2 * p : 2 * p + 2]

    def from_other_core(g):
        cc = g // PARTS
        first = (1 - core) * HALF + (g % PARTS) * SUB
        wait_bytes(stage_l.at[g], o_r.at[g])
        wait_bytes(stage_p.at[g], op_r.at[g])

        def one(a, carry):
            for p in range(2):
                place(cc, p, first + a, from_l[g, p, a].astype(F32))
            place_path(cc, first + a, from_p[g, a, 4:])
            return carry

        lax.fori_loop(0, SUB, one, 0)

    def write_out(cc):
        step = 8

        def one(i, carry):
            at = pl.multiple_of(i * step * ROWS, step * ROWS)
            for p in range(2):
                cols = slice((p * TILES + cc) * 128, (p * TILES + cc + 1) * 128)
                block = rows_f[cc, p, pl.ds(at, step * ROWS), :].astype(BF)
                out_l[pl.ds(i * step, step), :, cols] = block.reshape(step, ROWS, 128)
            return carry

        lax.fori_loop(0, r_dev // step, one, 0)
        for p in range(2):
            cols = slice((p * TILES + cc) * 128, (p * TILES + cc + 1) * 128)
            for q in range(2):
                out_p[q, :, cols] = rows_p[cc, p, q * ROWS : (q + 1) * ROWS, :]

    transpose(0)
    from_mate(0)
    from_mate(1)
    spread(2)
    own_plane(0)
    own_plane(1)
    transpose(1)
    from_mate(2)
    from_mate(3)
    z_arrivals(0)
    z_arrivals(1)
    other_plane(0)
    other_plane(1)
    transpose(2)
    from_mate(4)
    from_mate(5)
    own_plane(2)
    own_plane(3)
    build_factors()
    z_arrivals(2)
    z_arrivals(3)
    transform(0)
    transform(1)
    other_plane(2)
    other_plane(3)
    own_plane(4)
    own_plane(5)
    z_arrivals(4)
    z_arrivals(5)
    transform(2)
    transform(3)
    from_other_core(0)
    from_other_core(1)
    write_out(0)
    other_plane(4)
    other_plane(5)
    from_other_core(2)
    from_other_core(3)
    write_out(1)
    transform(4)
    transform(5)
    from_other_core(4)
    from_other_core(5)
    write_out(2)

    for cc in range(TILES):
        wait_bytes(send.at[cc, pl.ds(0, NKA - 1)], a2a_s.at[cc])
    wait_bytes(mixr.at[pl.ds(0, NROW - 1)], m_s)
    for g in range(CHUNKS):
        wait_bytes(gath.at[g, pl.ds(0, NROW - 1)], g_s.at[g])
        wait_bytes(stage_l.at[g], o_s.at[g])
        wait_bytes(stage_p.at[g], op_s.at[g])


def local(gauge, energies, kmesh, lattice, degeneracy, path):
    w = gauge.shape[2]
    nk = kmesh.shape[1]
    r_dev = lattice.shape[1]
    path_dev = path.shape[1] // NROW
    vmem = pl.BlockSpec(memory_space=pltpu.VMEM)
    dma = pltpu.SemaphoreType.DMA
    hbm = pl.BlockSpec(memory_space=pltpu.HBM)
    return pl.pallas_call(
        kernel,
        out_shape=(
            jax.ShapeDtypeStruct((r_dev, ROWS, 2 * w), BF),
            jax.ShapeDtypeStruct((path_dev, ROWS, 2 * w), F32),
        ),
        in_specs=[hbm] * 6,
        out_specs=(vmem, vmem),
        scratch_shapes=[
            pltpu.VMEM((2, w, w), BF),
            pltpu.VMEM((1, w), F32),
            pltpu.VMEM((3, nk), jnp.int32),
            pltpu.VMEM((3, r_dev), jnp.int32),
            pltpu.VMEM((1, r_dev), jnp.int32),
            pltpu.VMEM(path.shape, jnp.int32),
            dma((6,)),
            pltpu.VMEM((w, 2 * w), BF),
            pltpu.VMEM((2, w, w), BF),
            pltpu.VMEM((TILES, NKA, 2 * ROWS, 128), BF),
            pltpu.VMEM((TILES, NKA, 2 * ROWS, 128), BF),
            pltpu.VMEM((NKA * 2 * ROWS, 128), F32),
            pltpu.VMEM((CHUNKS, UNIT, NKA, 128), BF),
            pltpu.VMEM((CHUNKS, NROW, UNIT, NKA, 128), BF),
            pltpu.VMEM((4 * r_dev + 16, 2 * nk), BF),
            pltpu.VMEM((2, r_dev, 2 * nk), BF),
            pltpu.VMEM((NROW // 2, 8, nk), F32),
            pltpu.VMEM((NROW, 8, nk), F32),
            pltpu.VMEM((CHUNKS, 2, SUB, r_dev, 128), BF),
            pltpu.VMEM((CHUNKS, SUB, 8, 128), F32),
            pltpu.VMEM((CHUNKS, 2, SUB, r_dev, 128), BF),
            pltpu.VMEM((CHUNKS, SUB, 8, 128), F32),
            pltpu.VMEM((TILES, 2, r_dev * ROWS, 128), F32),
            pltpu.VMEM((TILES, 2, path_dev * ROWS, 128), F32),
            pltpu.VMEM((4, path_dev, 2 * nk), F32),
            dma((TILES,)),
            dma((TILES,)),
            dma((CHUNKS,)),
            dma((CHUNKS, NROW)),
            dma,
            dma,
            dma,
            dma,
            dma((CHUNKS,)),
            dma((CHUNKS,)),
            dma((CHUNKS,)),
            dma((CHUNKS,)),
        ],
        compiler_params=pltpu.CompilerParams(
            collective_id=0, has_side_effects=True, vmem_limit_bytes=48 << 20
        ),
    )(*[pltpu.with_memory_space_constraint(v, pltpu.HBM) for v in (gauge[0], energies, kmesh, lattice, degeneracy[None, :], path)])


def solution(mesh):
    return jax.shard_map(
        local,
        mesh=mesh,
        in_specs=(
            P(("ka", "row"), None, None, None),
            P(("ka", "row"), None),
            P(),
            P(None, "row"),
            P("row"),
            P(),
        ),
        out_specs=(P("row", "ka", None), P("row", "ka", None)),
        check_vma=False,
    )
```

```python
import functools
import math

import jax
import jax.numpy as jnp
from jax import lax
from jax.experimental import pallas as pl
from jax.experimental.pallas import tpu as pltpu
from jax.sharding import PartitionSpec as P

MESH = 12
PATH_DEN = 64
NKA = 16
NROW = 16
ROWS = 24
TILES = 3
HALF = ROWS // 2
PIECES = ((0, 0, 12), (1, 0, 6), (1, 6, 6), (2, 0, 4), (2, 4, 4), (2, 8, 4))
Y_FIRST = (1, 2, 3,)
ORDER = (
    (0,0), (1,0,0,0,1), (0,1), (1,0,0,-1,0), (1,0,1,0,0), (1,1,0,0,1), (1,2,0,0,1), (1,0,0,1,1),
    (1,0,1,0,1), (1,1,0,-1,0), (1,1,0,1,0), (0,2), (1,2,0,-1,0), (1,2,0,1,0), (1,3,0,0,1),
    (1,4,0,0,1), (1,5,0,0,1), (1,1,0,1,1), (1,0,1,-1,0), (1,2,0,1,1), (1,1,0,-1,1), (1,4,1,0,0),
    (1,5,1,0,0), (1,2,0,-1,1), (1,0,1,1,1), (1,3,0,1,0), (1,1,0,2,0), (1,4,1,0,1), (1,3,0,-1,0),
    (1,5,1,0,1), (1,4,0,-1,0), (1,3,0,1,1), (1,5,0,-1,0), (1,4,0,1,1), (1,2,0,2,0), (1,5,0,1,1),
    (1,3,0,-1,1), (1,1,0,2,1), (1,2,0,2,1), (1,4,1,-1,0), (1,5,1,-1,0), (2,0), (1,4,1,1,1),
    (1,3,0,2,0), (1,5,1,1,1), (1,3,0,2,1), (2,1), (2,2), (2,4), (2,5), (2,3),
)
CHUNKS = len(PIECES)

BF = jnp.bfloat16
F32 = jnp.float32


def kernel(
    gauge_h, energies_h, kmesh_h, lattice_h, degeneracy_h, path_h,
    out_l, out_p,
    gauge, energies, kmesh, lattice, degeneracy, path, in_s,
    at_ref, sc_ref, send, arrived, plain, other, gath, lmat, fpart, mixp, mixr,
    stage_l, stage_p, from_l, from_p, rows_f, rows_p, mix_f,
    a2a_s, a2a_r, g_s, g_r, f_s, f_r, m_s, m_r, o_s, o_r, op_s, op_r,
):
    loads = [
        pltpu.make_async_copy(src, dst, in_s.at[i])
        for i, (src, dst) in enumerate(
            (
                (energies_h, energies), (gauge_h, gauge), (kmesh_h, kmesh),
                (lattice_h, lattice), (degeneracy_h, degeneracy), (path_h, path),
            )
        )
    ]
    for load in loads:
        load.start()

    ka = lax.axis_index("ka")
    row = lax.axis_index("row")
    core = row % 2
    y = (row // 2) % 4
    zlo = row // 8
    x = ka // 4
    z = (ka % 4) * 2 + zlo
    turn = 2 * zlo - 1
    peers = [(dx, d) for d in (3, 2, 1, 0) for dx in (2, 1, 3, 0) if dx or d]

    def place_of(xx, zz):
        return (xx % 4) * 4 + zz // 2, (zz % 2) * 8 + row % 8
    mate = row + 1 - 2 * core

    def unit_of(z, yy, c):
        return z * 8 + yy * 2 + c

    yp = (y + 1) % 4
    ym = (y + 3) % 4
    yo = (y + 2) % 4
    zo = 1 - zlo

    barrier = pltpu.get_barrier_semaphore()
    for dx, d in peers:
        pl.semaphore_signal(
            barrier, inc=1, device_id=place_of(x + dx, (z + turn * d + 8) % 8),
            device_id_type=pl.DeviceIdType.MESH,
        )
    for i in range(1, NROW):
        pl.semaphore_signal(
            barrier, inc=1, device_id=(ka, (row + i) % NROW), device_id_type=pl.DeviceIdType.MESH
        )

    def remote(src, dst, ssem, rsem, dev):
        return pltpu.make_async_remote_copy(
            src_ref=src, dst_ref=dst, send_sem=ssem, recv_sem=rsem,
            device_id=dev, device_id_type=pl.DeviceIdType.MESH,
        )

    def wait_bytes(ref, sem):
        pltpu.make_async_copy(ref, ref, sem).wait()

    loads[0].wait()
    loads[1].wait()
    w = gauge.shape[1]
    e_col = jnp.transpose(jnp.broadcast_to(energies[...], (128, w)))
    e_full = jnp.concatenate([e_col] * (w // 128), 1)
    for p in range(2):
        u = gauge[p].astype(F32)
        at_ref[:, p * w : (p + 1) * w] = jnp.transpose(u).astype(BF)
        sc_ref[p] = (e_full * u).astype(BF)

    def rotate(cc):
        cols = slice(cc * 128, cc * 128 + 128)
        sr = sc_ref[0, :, cols]
        si = sc_ref[1, :, cols]
        rhs = jnp.concatenate(
            [jnp.concatenate([sr, si], 1), jnp.concatenate([si, -sr], 1)], 0
        )
        h = jnp.dot(at_ref[...], rhs, preferred_element_type=F32)
        for j in range(NKA):
            both = jnp.concatenate(
                [h[j * ROWS : (j + 1) * ROWS, :128], h[j * ROWS : (j + 1) * ROWS, 128:]], 0
            )
            send[cc, j] = both.astype(BF)

    def spread(cc):
        for dx, d in peers:
            to = place_of(x + dx, (z + turn * (0, 1, -2, 3)[d] + 8) % 8)
            remote(
                send.at[cc, to[0]], arrived.at[cc, x * 4 + d], a2a_s.at[cc], a2a_r.at[cc], to
            ).start()
        arrived[cc, pl.ds(x * 4, 1)] = send[cc, pl.ds(ka, 1)]

    rotate(0)
    pl.semaphore_wait(barrier, NKA - 1 + NROW - 1)
    spread(0)
    rotate(1)
    spread(1)
    rotate(2)
    spread(2)

    for load in loads[2:]:
        load.wait()
    nk = kmesh.shape[1]
    r_dev = lattice.shape[1]
    np_all = path.shape[1]

    def pad_rows(a):
        return jnp.concatenate([a.astype(F32), jnp.zeros((13, a.shape[1]), F32)], 0).astype(BF)

    lat = pad_rows(lattice[...])
    at_k = lax.broadcasted_iota(jnp.int32, (nk, nk), 0)
    pos = lax.broadcasted_iota(jnp.int32, (8, nk), 1)
    pos_z = pos >> 7
    from_z = ((ka % 4) * 2 + pos_z + (2 * pos_z - 1) * (pos & 3) + 8) & 7
    source = ((((pos >> 2) & 3) * 4 + (from_z >> 1)) * NROW) + (from_z & 1) * 8 + ((pos >> 4) & 7)
    order = jnp.where(at_k == source[:1], 1.0, 0.0).astype(BF)
    km = jnp.dot(pad_rows(kmesh[...]), order, preferred_element_type=F32).astype(BF)
    dims = (((0,), (0,)), ((), ()))
    wind = lax.dot_general(lat, km, dims, preferred_element_type=F32).astype(jnp.int32)
    wind = jnp.mod(wind + 23 * MESH, MESH)
    angle = wind.astype(F32) * (2.0 * math.pi / MESH)
    fcos = jnp.cos(angle).astype(BF)
    fsin = jnp.sin(angle).astype(BF)
    fpart[0, :, :nk] = fcos
    fpart[0, :, nk:] = fsin
    f_copy = remote(fpart.at[0], fpart.at[1], f_s, f_r, (ka, mate))
    f_copy.start()
    wind_p = lax.dot_general(pad_rows(path[...]), lat, dims, preferred_element_type=F32)
    wind_p = jnp.mod(wind_p.astype(jnp.int32) + 24 * PATH_DEN, PATH_DEN)
    angle_p = wind_p.astype(F32) * (2.0 * math.pi / PATH_DEN)
    weights = 1.0 / degeneracy[...].astype(F32)
    pcos = (jnp.cos(angle_p) * weights).astype(BF)
    psin = (jnp.sin(angle_p) * weights).astype(BF)
    pboth = jnp.concatenate([pcos, psin], 0)
    mc = jnp.dot(pboth, fcos, preferred_element_type=F32)
    ms = jnp.dot(pboth, fsin, preferred_element_type=F32)
    m_re = mc[:np_all] + ms[np_all:]
    m_im = mc[np_all:] - ms[:np_all]
    per_chip = np_all // (NROW // 2)
    for p in range(NROW // 2):
        mixp[p, :per_chip] = m_re[p * per_chip : (p + 1) * per_chip]
        mixp[p, per_chip:] = m_im[p * per_chip : (p + 1) * per_chip]
    for i in range(1, NROW):
        to = (row + i) % NROW
        remote(mixp.at[to // 2], mixr.at[row], m_s, m_r, (ka, to)).start()
    mixr[pl.ds(row, 1)] = mixp[pl.ds(row // 2, 1)]

    def take_tile(cc):
        wait_bytes(arrived.at[cc, pl.ds(0, NKA - 1)], a2a_r.at[cc])
        plain[...] = arrived[cc].reshape(NKA * 2 * ROWS, 128).astype(F32)
        for g, (tile, first, rows) in enumerate(PIECES):
            if tile != cc:
                continue
            for half, dst in ((1 - core, other[g]), (core, gath[g].at[row])):
                for p in range(2):
                    for a in range(rows):
                        at = p * ROWS + first + a + half * HALF
                        values = plain[pl.ds(at, NKA, stride=2 * ROWS), :]
                        dst[p * rows + a] = values.astype(BF)
                if dst is other[g]:
                    remote(
                        other[g], gath[g].at[row], g_s.at[g], g_r.at[g, row], (ka, mate)
                    ).start()
            pass_on(g, 0, 0, 0)

    def unit_at(plane, dy, r):
        return unit_of((zlo + plane) % 2, (y + dy + 4) % 4, (core + r) % 2)

    def pass_on(g, plane, dy, r):
        u = unit_at(plane, dy, r)
        y_first = g in Y_FIRST
        to = []
        if plane == 0 or not y_first:
            if dy == 0 or (dy == -1 and r == 0):
                to.append(unit_of(zlo, yp, core))
            if dy == 0 or (dy == 1 and r == 1):
                to.append(unit_of(zlo, ym, core))
        if plane == 0 and (y_first or dy == 0):
            to.append(unit_of(zo, y, core))
        for t in to:
            remote(gath[g].at[u], gath[g].at[u], g_s.at[g], g_r.at[g, u], (ka, t)).start()

    def landed(g, plane, dy, r):
        u = unit_at(plane, dy, r)
        wait_bytes(gath[g].at[u], g_r.at[g, u])

    def build_factors():
        wait_bytes(mixr.at[pl.ds(0, NROW - 1)], m_r)
        f_copy.wait()
        for s in range(2):
            at = s * 2 * r_dev
            c_part = fpart[s, :, :nk]
            s_part = fpart[s, :, nk:]
            lmat[at : at + r_dev, :nk] = c_part
            lmat[at : at + r_dev, nk:] = s_part
            lmat[at + r_dev : at + 2 * r_dev, :nk] = -s_part
            lmat[at + r_dev : at + 2 * r_dev, nk:] = c_part
        total = mixr[0]
        for i in range(1, NROW):
            total = total + mixr[i]
        m_r4 = total[:per_chip]
        m_i4 = total[per_chip:]
        wide = jnp.concatenate(
            [jnp.concatenate([m_r4, -m_i4], 1), jnp.concatenate([m_i4, m_r4], 1)], 0
        )
        own_q = per_chip // 2
        for i in range(4):
            mix_f[i] = wide[i * own_q : (i + 1) * own_q]
        wide = jnp.concatenate([mix_f[2 * p + c] for c in (core, 1 - core) for p in range(2)], 0)
        high = wide.astype(BF)
        low = (wide - high.astype(F32)).astype(BF)
        lmat[4 * r_dev :, :] = jnp.concatenate([high.astype(F32), low.astype(F32)], 0).astype(BF)

    scale = 1.0 / nk

    def transform(g):
        cc, first, rows = PIECES[g]

        def one(i, carry):
            a = 2 * i
            re0 = gath[g][:, a].reshape(nk, 128)
            re1 = gath[g][:, a + 1].reshape(nk, 128)
            im0 = gath[g][:, rows + a].reshape(nk, 128)
            im1 = gath[g][:, rows + a + 1].reshape(nk, 128)
            both = jnp.concatenate(
                [jnp.concatenate([re0, re1], 1), jnp.concatenate([im0, im1], 1)], 0
            )
            product = jnp.dot(lmat[...], both, preferred_element_type=F32) * scale
            for b in range(2):
                v = product[:, b * 128 : b * 128 + 128]
                for p in range(2):
                    place(cc, p, core * HALF + first + a + b, v[p * r_dev : (p + 1) * r_dev])
                    stage_l[g][p, a + b] = v[(2 + p) * r_dev : (3 + p) * r_dev].astype(BF)
                vp = v[4 * r_dev : 4 * r_dev + 8] + v[4 * r_dev + 8 :]
                place_path(cc, core * HALF + first + a + b, vp[:4])
                stage_p[g][a + b] = vp
            return carry

        lax.fori_loop(0, rows // 2, one, 0)
        remote(stage_l[g], from_l[g], o_s.at[g], o_r.at[g], (ka, mate)).start()
        remote(stage_p[g], from_p[g], op_s.at[g], op_r.at[g], (ka, mate)).start()

    def place(cc, p, a, value):
        rows_f[cc, p, pl.ds(a, r_dev, stride=ROWS), :] = value

    def place_path(cc, a, value):
        for p in range(2):
            rows_p[cc, p, pl.ds(a, 2, stride=ROWS), :] = value[2 * p : 2 * p + 2]

    def from_other_core(g):
        cc, first, rows = PIECES[g]
        start = (1 - core) * HALF + first
        wait_bytes(stage_l[g], o_r.at[g])
        wait_bytes(stage_p[g], op_r.at[g])

        def one(a, carry):
            for p in range(2):
                place(cc, p, start + a, from_l[g][p, a].astype(F32))
            place_path(cc, start + a, from_p[g][a, 4:])
            return carry

        lax.fori_loop(0, rows, one, 0)

    def write_out(cc):
        step = 8

        def one(i, carry):
            at = pl.multiple_of(i * step * ROWS, step * ROWS)
            for p in range(2):
                cols = slice((p * TILES + cc) * 128, (p * TILES + cc + 1) * 128)
                block = rows_f[cc, p, pl.ds(at, step * ROWS), :].astype(BF)
                out_l[pl.ds(i * step, step), :, cols] = block.reshape(step, ROWS, 128)
            return carry

        lax.fori_loop(0, r_dev // step, one, 0)
        for p in range(2):
            cols = slice((p * TILES + cc) * 128, (p * TILES + cc + 1) * 128)
            for q in range(2):
                out_p[q, :, cols] = rows_p[cc, p, q * ROWS : (q + 1) * ROWS, :]

    everything = [(pn, dy, r) for pn in range(2) for dy in (0, -1, 1, 2) for r in range(2)][1:]
    pending = {g: list(everything) for g in range(CHUNKS)}
    left = {cc: sum(t == cc for t, _, _ in PIECES) for cc in range(TILES)}

    def finish(g):
        from_other_core(g)
        left[PIECES[g][0]] -= 1
        if left[PIECES[g][0]] == 0:
            write_out(PIECES[g][0])

    last = None
    for what, g, *unit in ORDER:
        if what == 0:
            take_tile(g)
        elif what == 1:
            landed(g, *unit)
            pending[g].remove(tuple(unit))
            pass_on(g, *unit)
        else:
            if last is None:
                build_factors()
            for rest in pending[g]:
                landed(g, *rest)
            transform(g)
            if last is not None:
                finish(last)
            last = g
    finish(last)

    for cc in range(TILES):
        wait_bytes(send.at[cc, pl.ds(0, NKA - 1)], a2a_s.at[cc])
    wait_bytes(mixr.at[pl.ds(0, NROW - 1)], m_s)
    for g in range(CHUNKS):
        wait_bytes(gath[g].at[pl.ds(0, NROW - 1)], g_s.at[g])
        wait_bytes(stage_l[g], o_s.at[g])
        wait_bytes(stage_p[g], op_s.at[g])


def local(gauge, energies, kmesh, lattice, degeneracy, path):
    w = gauge.shape[2]
    nk = kmesh.shape[1]
    r_dev = lattice.shape[1]
    path_dev = path.shape[1] // NROW
    vmem = pl.BlockSpec(memory_space=pltpu.VMEM)
    dma = pltpu.SemaphoreType.DMA
    hbm = pl.BlockSpec(memory_space=pltpu.HBM)
    rows = [n for _, _, n in PIECES]
    return pl.pallas_call(
        kernel,
        out_shape=(
            jax.ShapeDtypeStruct((r_dev, ROWS, 2 * w), BF),
            jax.ShapeDtypeStruct((path_dev, ROWS, 2 * w), F32),
        ),
        in_specs=[hbm] * 6,
        out_specs=(vmem, vmem),
        scratch_shapes=[
            pltpu.VMEM((2, w, w), BF),
            pltpu.VMEM((1, w), F32),
            pltpu.VMEM((3, nk), jnp.int32),
            pltpu.VMEM((3, r_dev), jnp.int32),
            pltpu.VMEM((1, r_dev), jnp.int32),
            pltpu.VMEM(path.shape, jnp.int32),
            dma((6,)),
            pltpu.VMEM((w, 2 * w), BF),
            pltpu.VMEM((2, w, w), BF),
            pltpu.VMEM((TILES, NKA, 2 * ROWS, 128), BF),
            pltpu.VMEM((TILES, NKA, 2 * ROWS, 128), BF),
            pltpu.VMEM((NKA * 2 * ROWS, 128), F32),
            [pltpu.VMEM((2 * n, NKA, 128), BF) for n in rows],
            [pltpu.VMEM((NROW, 2 * n, NKA, 128), BF) for n in rows],
            pltpu.VMEM((4 * r_dev + 16, 2 * nk), BF),
            pltpu.VMEM((2, r_dev, 2 * nk), BF),
            pltpu.VMEM((NROW // 2, 8, nk), F32),
            pltpu.VMEM((NROW, 8, nk), F32),
            [pltpu.VMEM((2, n, r_dev, 128), BF) for n in rows],
            [pltpu.VMEM((n, 8, 128), F32) for n in rows],
            [pltpu.VMEM((2, n, r_dev, 128), BF) for n in rows],
            [pltpu.VMEM((n, 8, 128), F32) for n in rows],
            pltpu.VMEM((TILES, 2, r_dev * ROWS, 128), F32),
            pltpu.VMEM((TILES, 2, path_dev * ROWS, 128), F32),
            pltpu.VMEM((4, path_dev, 2 * nk), F32),
            dma((TILES,)),
            dma((TILES,)),
            dma((CHUNKS,)),
            dma((CHUNKS, NROW)),
            dma,
            dma,
            dma,
            dma,
            dma((CHUNKS,)),
            dma((CHUNKS,)),
            dma((CHUNKS,)),
            dma((CHUNKS,)),
        ],
        compiler_params=pltpu.CompilerParams(
            collective_id=0, has_side_effects=True, vmem_limit_bytes=48 << 20
        ),
    )(
        *[
            pltpu.with_memory_space_constraint(v, pltpu.HBM)
            for v in (gauge[0], energies, kmesh, lattice, degeneracy[None, :], path)
        ]
    )


def solution(mesh):
    return jax.shard_map(
        local,
        mesh=mesh,
        in_specs=(
            P(("ka", "row"), None, None, None),
            P(("ka", "row"), None),
            P(),
            P(None, "row"),
            P("row"),
            P(),
        ),
        out_specs=(P("row", "ka", None), P("row", "ka", None)),
        check_vma=False,
    )
```

```python
import math

import jax
import jax.numpy as jnp
from jax import lax
from jax.experimental import pallas as pl
from jax.experimental.pallas import tpu as pltpu
from jax.sharding import PartitionSpec as P

MESH = 12
PATH_DEN = 64
NKA = 16
NROW = 16
ROWS = 24
TILES = 3
HALF = ROWS // 2
BLOCKS = ((0, 0, 4), (0, 4, 4), (0, 8, 4), (1, 0, 12), (2, 0, 12))
PIECES = ((0, 0, 4), (0, 4, 4), (0, 8, 4), (1, 0, 6), (1, 6, 6), (2, 0, 6), (2, 6, 6))
Y_FIRST = (1, 4, 5,)
ORDER = (
    (0,0), (0,1), (1,0,0,0,1), (1,0,0,-1,0), (0,2), (1,1,0,0,1), (1,0,1,0,0), (1,1,0,-1,0),
    (1,1,0,1,0), (1,2,0,0,1), (1,0,0,1,1), (1,0,1,0,1), (1,2,1,0,0), (1,2,0,-1,0), (1,1,0,1,1),
    (1,1,0,-1,1), (0,3), (1,0,1,-1,0), (1,2,0,1,1), (1,1,0,2,0), (1,2,1,0,1), (1,3,0,0,1),
    (1,4,0,0,1), (1,0,1,1,1), (1,2,1,-1,0), (1,1,0,2,1), (1,3,1,0,0), (0,4), (1,3,0,-1,0),
    (1,4,0,1,0), (1,5,0,0,1), (1,6,0,0,1), (1,4,0,-1,0), (1,3,1,0,1), (1,2,1,1,1), (1,3,0,1,1),
    (2,1), (1,4,0,1,1), (1,4,0,-1,1), (2,0), (1,6,1,0,0), (1,3,1,-1,0), (1,5,0,1,0),
    (1,5,0,-1,0), (1,6,0,-1,0), (1,6,1,0,1), (1,5,0,1,1), (1,6,0,1,1), (1,5,0,-1,1),
    (1,3,1,1,1), (2,2), (1,4,0,2,0), (1,4,0,2,1), (1,6,1,-1,0), (1,6,1,1,1), (1,5,0,2,0),
    (1,5,0,2,1), (2,4), (2,3), (2,6), (2,5),
)
CHUNKS = len(PIECES)

BF = jnp.bfloat16
F32 = jnp.float32


def kernel(
    gauge_h, energies_h, kmesh_h, lattice_h, degeneracy_h, path_h,
    out_l, out_p,
    gauge, energies, kmesh, lattice, degeneracy, path, in_s,
    at_ref, sc_ref, send, arrived, plain, other, gath, lmat, fpart, mixp, mixr,
    stage_l, stage_p, from_l, from_p, rows_f, rows_p, mix_f,
    a2a_s, a2a_r, g_s, g_r, f_s, f_r, m_s, m_r, o_s, o_r, op_s, op_r,
):
    loads = [
        pltpu.make_async_copy(src, dst, in_s.at[i])
        for i, (src, dst) in enumerate(
            (
                (energies_h, energies), (gauge_h, gauge), (kmesh_h, kmesh),
                (lattice_h, lattice), (degeneracy_h, degeneracy), (path_h, path),
            )
        )
    ]
    for load in loads:
        load.start()

    ka = lax.axis_index("ka")
    row = lax.axis_index("row")
    core = row % 2
    y = (row // 2) % 4
    zlo = row // 8
    x = ka // 4
    z = (ka % 4) * 2 + zlo
    turn = 2 * zlo - 1
    peers = [(dx, d) for d in (3, 2, 1, 0) for dx in (2, 1, 3, 0) if dx or d]

    def place_of(xx, zz):
        return (xx % 4) * 4 + zz // 2, (zz % 2) * 8 + row % 8
    mate = row + 1 - 2 * core

    def unit_of(z, yy, c):
        return z * 8 + yy * 2 + c

    yp = (y + 1) % 4
    ym = (y + 3) % 4
    yo = (y + 2) % 4
    zo = 1 - zlo

    barrier = pltpu.get_barrier_semaphore()
    for dx, d in peers:
        pl.semaphore_signal(
            barrier, inc=1, device_id=place_of(x + dx, (z + turn * d + 8) % 8),
            device_id_type=pl.DeviceIdType.MESH,
        )
    for i in range(1, NROW):
        pl.semaphore_signal(
            barrier, inc=1, device_id=(ka, (row + i) % NROW), device_id_type=pl.DeviceIdType.MESH
        )

    def remote(src, dst, ssem, rsem, dev):
        return pltpu.make_async_remote_copy(
            src_ref=src, dst_ref=dst, send_sem=ssem, recv_sem=rsem,
            device_id=dev, device_id_type=pl.DeviceIdType.MESH,
        )

    def wait_bytes(ref, sem):
        pltpu.make_async_copy(ref, ref, sem).wait()

    loads[0].wait()
    loads[1].wait()
    w = gauge.shape[1]
    e_col = jnp.transpose(jnp.broadcast_to(energies[...], (128, w)))
    e_full = jnp.concatenate([e_col] * (w // 128), 1)
    for p in range(2):
        u = gauge[p].astype(F32)
        at_ref[:, p * w : (p + 1) * w] = jnp.transpose(u).astype(BF)
        sc_ref[p] = (e_full * u).astype(BF)

    def rotate(cc):
        cols = slice(cc * 128, cc * 128 + 128)
        sr = sc_ref[0, :, cols]
        si = sc_ref[1, :, cols]
        rhs = jnp.concatenate(
            [jnp.concatenate([sr, si], 1), jnp.concatenate([si, -sr], 1)], 0
        )
        h = jnp.dot(at_ref[...], rhs, preferred_element_type=F32)
        for j in range(NKA):
            groups = [
                h[j * ROWS + t * 8 : j * ROWS + t * 8 + 8, p * 128 : p * 128 + 128]
                for t in range(ROWS // 8)
                for p in range(2)
            ]
            send[cc, j] = jnp.concatenate(groups, 0).astype(BF)

    def lines_of(i):
        return pl.ds(BLOCKS[i][1] * 4, BLOCKS[i][2] * 4)

    def spread(cc):
        for i, (tile, _, _) in enumerate(BLOCKS):
            if tile != cc:
                continue
            lines = lines_of(i)
            for dx, d in peers:
                to = place_of(x + dx, (z + turn * (0, 1, -2, 3)[d] + 8) % 8)
                remote(
                    send.at[cc, to[0], lines], arrived.at[cc, x * 4 + d, lines],
                    a2a_s.at[i], a2a_r.at[i], to,
                ).start()
        arrived[cc, pl.ds(x * 4, 1)] = send[cc, pl.ds(ka, 1)]

    rotate(0)
    pl.semaphore_wait(barrier, NKA - 1 + NROW - 1)
    spread(0)
    rotate(1)
    spread(1)
    rotate(2)
    spread(2)

    for load in loads[2:]:
        load.wait()
    nk = kmesh.shape[1]
    r_dev = lattice.shape[1]
    np_all = path.shape[1]

    def pad_rows(a):
        return jnp.concatenate([a.astype(F32), jnp.zeros((13, a.shape[1]), F32)], 0).astype(BF)

    lat = pad_rows(lattice[...])
    at_k = lax.broadcasted_iota(jnp.int32, (nk, nk), 0)
    pos = lax.broadcasted_iota(jnp.int32, (8, nk), 1)
    pos_z = pos >> 7
    from_z = ((ka % 4) * 2 + pos_z + (2 * pos_z - 1) * (pos & 3) + 8) & 7
    source = ((((pos >> 2) & 3) * 4 + (from_z >> 1)) * NROW) + (from_z & 1) * 8 + ((pos >> 4) & 7)
    order = jnp.where(at_k == source[:1], 1.0, 0.0).astype(BF)
    km = jnp.dot(pad_rows(kmesh[...]), order, preferred_element_type=F32).astype(BF)
    dims = (((0,), (0,)), ((), ()))
    wind = lax.dot_general(lat, km, dims, preferred_element_type=F32).astype(jnp.int32)
    wind = jnp.mod(wind + 23 * MESH, MESH)
    angle = wind.astype(F32) * (2.0 * math.pi / MESH)
    fcos = jnp.cos(angle).astype(BF)
    fsin = jnp.sin(angle).astype(BF)
    fpart[0, :, :nk] = fcos
    fpart[0, :, nk:] = fsin
    f_copy = remote(fpart.at[0], fpart.at[1], f_s, f_r, (ka, mate))
    f_copy.start()
    wind_p = lax.dot_general(pad_rows(path[...]), lat, dims, preferred_element_type=F32)
    wind_p = jnp.mod(wind_p.astype(jnp.int32) + 24 * PATH_DEN, PATH_DEN)
    angle_p = wind_p.astype(F32) * (2.0 * math.pi / PATH_DEN)
    weights = 1.0 / degeneracy[...].astype(F32)
    pcos = (jnp.cos(angle_p) * weights).astype(BF)
    psin = (jnp.sin(angle_p) * weights).astype(BF)
    pboth = jnp.concatenate([pcos, psin], 0)
    mc = jnp.dot(pboth, fcos, preferred_element_type=F32)
    ms = jnp.dot(pboth, fsin, preferred_element_type=F32)
    m_re = mc[:np_all] + ms[np_all:]
    m_im = mc[np_all:] - ms[:np_all]
    per_chip = np_all // (NROW // 2)
    for p in range(NROW // 2):
        mixp[p, :per_chip] = m_re[p * per_chip : (p + 1) * per_chip]
        mixp[p, per_chip:] = m_im[p * per_chip : (p + 1) * per_chip]
    for i in range(1, NROW):
        to = (row + i) % NROW
        remote(mixp.at[to // 2], mixr.at[row], m_s, m_r, (ka, to)).start()
    mixr[pl.ds(row, 1)] = mixp[pl.ds(row // 2, 1)]

    def take_block(i):
        cc, start, count = BLOCKS[i]
        lines = count * 4
        wait_bytes(arrived.at[cc, pl.ds(0, NKA - 1), lines_of(i)], a2a_r.at[i])
        block = arrived[cc, :, lines_of(i)]
        plain[: NKA * lines] = block.reshape(NKA * lines, 128).astype(F32)
        for g, (tile, first, rows) in enumerate(PIECES):
            if tile != cc or not start <= first < start + count:
                continue
            for half, dst in ((1 - core, other[g]), (core, gath[g].at[row])):
                for p in range(2):
                    for a in range(rows):
                        at = first + a - start
                        at = (at // 4) * 16 + p * 8 + at % 4 + half * 4
                        values = plain[pl.ds(at, NKA, stride=lines), :]
                        dst[p * rows + a] = values.astype(BF)
                if dst is other[g]:
                    remote(
                        other[g], gath[g].at[row], g_s.at[g], g_r.at[g, row], (ka, mate)
                    ).start()
            pass_on(g, 0, 0, 0)

    def unit_at(plane, dy, r):
        return unit_of((zlo + plane) % 2, (y + dy + 4) % 4, (core + r) % 2)

    def pass_on(g, plane, dy, r):
        u = unit_at(plane, dy, r)
        y_first = g in Y_FIRST
        to = []
        if plane == 0 or not y_first:
            if dy == 0 or (dy == -1 and r == 0):
                to.append(unit_of(zlo, yp, core))
            if dy == 0 or (dy == 1 and r == 1):
                to.append(unit_of(zlo, ym, core))
        if plane == 0 and (y_first or dy == 0):
            to.append(unit_of(zo, y, core))
        for t in to:
            remote(gath[g].at[u], gath[g].at[u], g_s.at[g], g_r.at[g, u], (ka, t)).start()

    def landed(g, plane, dy, r):
        u = unit_at(plane, dy, r)
        wait_bytes(gath[g].at[u], g_r.at[g, u])

    def build_factors():
        wait_bytes(mixr.at[pl.ds(0, NROW - 1)], m_r)
        f_copy.wait()
        for s in range(2):
            at = s * 2 * r_dev
            c_part = fpart[s, :, :nk]
            s_part = fpart[s, :, nk:]
            lmat[at : at + r_dev, :nk] = c_part
            lmat[at : at + r_dev, nk:] = s_part
            lmat[at + r_dev : at + 2 * r_dev, :nk] = -s_part
            lmat[at + r_dev : at + 2 * r_dev, nk:] = c_part
        total = mixr[0]
        for i in range(1, NROW):
            total = total + mixr[i]
        m_r4 = total[:per_chip]
        m_i4 = total[per_chip:]
        wide = jnp.concatenate(
            [jnp.concatenate([m_r4, -m_i4], 1), jnp.concatenate([m_i4, m_r4], 1)], 0
        )
        own_q = per_chip // 2
        for i in range(4):
            mix_f[i] = wide[i * own_q : (i + 1) * own_q]
        wide = jnp.concatenate([mix_f[2 * p + c] for c in (core, 1 - core) for p in range(2)], 0)
        high = wide.astype(BF)
        low = (wide - high.astype(F32)).astype(BF)
        lmat[4 * r_dev :, :] = jnp.concatenate([high.astype(F32), low.astype(F32)], 0).astype(BF)

    scale = 1.0 / nk

    def transform(g):
        cc, first, rows = PIECES[g]

        def one(i, carry):
            a = 2 * i
            re0 = gath[g][:, a].reshape(nk, 128)
            re1 = gath[g][:, a + 1].reshape(nk, 128)
            im0 = gath[g][:, rows + a].reshape(nk, 128)
            im1 = gath[g][:, rows + a + 1].reshape(nk, 128)
            both = jnp.concatenate(
                [jnp.concatenate([re0, re1], 1), jnp.concatenate([im0, im1], 1)], 0
            )
            product = jnp.dot(lmat[...], both, preferred_element_type=F32) * scale
            for b in range(2):
                v = product[:, b * 128 : b * 128 + 128]
                for p in range(2):
                    place(cc, p, core, first + a + b, v[p * r_dev : (p + 1) * r_dev])
                    stage_l[g][p, a + b] = v[(2 + p) * r_dev : (3 + p) * r_dev].astype(BF)
                vp = v[4 * r_dev : 4 * r_dev + 8] + v[4 * r_dev + 8 :]
                place_path(cc, core, first + a + b, vp[:4])
                stage_p[g][a + b] = vp
            return carry

        lax.fori_loop(0, rows // 2, one, 0)
        remote(stage_l[g], from_l[g], o_s.at[g], o_r.at[g], (ka, mate)).start()
        remote(stage_p[g], from_p[g], op_s.at[g], op_r.at[g], (ka, mate)).start()

    def row_at(half, a):
        return (a // 4) * 8 + half * 4 + a % 4

    def place(cc, p, half, a, value):
        rows_f[cc, p, pl.ds(row_at(half, a), r_dev, stride=ROWS), :] = value

    def place_path(cc, half, a, value):
        for p in range(2):
            rows_p[cc, p, pl.ds(row_at(half, a), 2, stride=ROWS), :] = value[2 * p : 2 * p + 2]

    def from_other_core(g):
        cc, first, rows = PIECES[g]
        wait_bytes(stage_l[g], o_r.at[g])
        wait_bytes(stage_p[g], op_r.at[g])

        def one(a, carry):
            for p in range(2):
                place(cc, p, 1 - core, first + a, from_l[g][p, a].astype(F32))
            place_path(cc, 1 - core, first + a, from_p[g][a, 4:])
            return carry

        lax.fori_loop(0, rows, one, 0)

    def write_out(cc):
        step = 8

        def one(i, carry):
            at = pl.multiple_of(i * step * ROWS, step * ROWS)
            for p in range(2):
                cols = slice((p * TILES + cc) * 128, (p * TILES + cc + 1) * 128)
                block = rows_f[cc, p, pl.ds(at, step * ROWS), :].astype(BF)
                out_l[pl.ds(i * step, step), :, cols] = block.reshape(step, ROWS, 128)
            return carry

        lax.fori_loop(0, r_dev // step, one, 0)
        for p in range(2):
            cols = slice((p * TILES + cc) * 128, (p * TILES + cc + 1) * 128)
            for q in range(2):
                out_p[q, :, cols] = rows_p[cc, p, q * ROWS : (q + 1) * ROWS, :]

    everything = [(pn, dy, r) for pn in range(2) for dy in (0, -1, 1, 2) for r in range(2)][1:]
    pending = {g: list(everything) for g in range(CHUNKS)}
    left = {cc: sum(t == cc for t, _, _ in PIECES) for cc in range(TILES)}

    def finish(g):
        from_other_core(g)
        left[PIECES[g][0]] -= 1
        if left[PIECES[g][0]] == 0:
            write_out(PIECES[g][0])

    last = None
    for what, g, *unit in ORDER:
        if what == 0:
            take_block(g)
        elif what == 1:
            landed(g, *unit)
            pending[g].remove(tuple(unit))
            pass_on(g, *unit)
        else:
            if last is None:
                build_factors()
            for rest in pending[g]:
                landed(g, *rest)
            transform(g)
            if last is not None:
                finish(last)
            last = g
    finish(last)

    for i, (cc, _, _) in enumerate(BLOCKS):
        wait_bytes(send.at[cc, pl.ds(0, NKA - 1), lines_of(i)], a2a_s.at[i])
    wait_bytes(mixr.at[pl.ds(0, NROW - 1)], m_s)
    for g in range(CHUNKS):
        wait_bytes(gath[g].at[pl.ds(0, NROW - 1)], g_s.at[g])
        wait_bytes(stage_l[g], o_s.at[g])
        wait_bytes(stage_p[g], op_s.at[g])


def local(gauge, energies, kmesh, lattice, degeneracy, path):
    w = gauge.shape[2]
    nk = kmesh.shape[1]
    r_dev = lattice.shape[1]
    path_dev = path.shape[1] // NROW
    vmem = pl.BlockSpec(memory_space=pltpu.VMEM)
    dma = pltpu.SemaphoreType.DMA
    hbm = pl.BlockSpec(memory_space=pltpu.HBM)
    rows = [n for _, _, n in PIECES]
    return pl.pallas_call(
        kernel,
        out_shape=(
            jax.ShapeDtypeStruct((r_dev, ROWS, 2 * w), BF),
            jax.ShapeDtypeStruct((path_dev, ROWS, 2 * w), F32),
        ),
        in_specs=[hbm] * 6,
        out_specs=(vmem, vmem),
        scratch_shapes=[
            pltpu.VMEM((2, w, w), BF),
            pltpu.VMEM((1, w), F32),
            pltpu.VMEM((3, nk), jnp.int32),
            pltpu.VMEM((3, r_dev), jnp.int32),
            pltpu.VMEM((1, r_dev), jnp.int32),
            pltpu.VMEM(path.shape, jnp.int32),
            dma((6,)),
            pltpu.VMEM((w, 2 * w), BF),
            pltpu.VMEM((2, w, w), BF),
            pltpu.VMEM((TILES, NKA, 2 * ROWS, 128), BF),
            pltpu.VMEM((TILES, NKA, 2 * ROWS, 128), BF),
            pltpu.VMEM((NKA * 2 * ROWS, 128), F32),
            [pltpu.VMEM((2 * n, NKA, 128), BF) for n in rows],
            [pltpu.VMEM((NROW, 2 * n, NKA, 128), BF) for n in rows],
            pltpu.VMEM((4 * r_dev + 16, 2 * nk), BF),
            pltpu.VMEM((2, r_dev, 2 * nk), BF),
            pltpu.VMEM((NROW // 2, 8, nk), F32),
            pltpu.VMEM((NROW, 8, nk), F32),
            [pltpu.VMEM((2, n, r_dev, 128), BF) for n in rows],
            [pltpu.VMEM((n, 8, 128), F32) for n in rows],
            [pltpu.VMEM((2, n, r_dev, 128), BF) for n in rows],
            [pltpu.VMEM((n, 8, 128), F32) for n in rows],
            pltpu.VMEM((TILES, 2, r_dev * ROWS, 128), F32),
            pltpu.VMEM((TILES, 2, path_dev * ROWS, 128), F32),
            pltpu.VMEM((4, path_dev, 2 * nk), F32),
            dma((len(BLOCKS),)),
            dma((len(BLOCKS),)),
            dma((CHUNKS,)),
            dma((CHUNKS, NROW)),
            dma,
            dma,
            dma,
            dma,
            dma((CHUNKS,)),
            dma((CHUNKS,)),
            dma((CHUNKS,)),
            dma((CHUNKS,)),
        ],
        compiler_params=pltpu.CompilerParams(
            collective_id=0, has_side_effects=True, vmem_limit_bytes=48 << 20
        ),
    )(
        *[
            pltpu.with_memory_space_constraint(v, pltpu.HBM)
            for v in (gauge[0], energies, kmesh, lattice, degeneracy[None, :], path)
        ]
    )


def solution(mesh):
    return jax.shard_map(
        local,
        mesh=mesh,
        in_specs=(
            P(("ka", "row"), None, None, None),
            P(("ka", "row"), None),
            P(),
            P(None, "row"),
            P("row"),
            P(),
        ),
        out_specs=(P("row", "ka", None), P("row", "ka", None)),
        check_vma=False,
    )
```

```python
import math

import jax
import jax.numpy as jnp
from jax import lax
from jax.experimental import pallas as pl
from jax.experimental.pallas import tpu as pltpu
from jax.sharding import PartitionSpec as P

MESH = 12
PATH_DEN = 64
NKA = 16
NROW = 16
ROWS = 24
TILES = 3
HALF = ROWS // 2
BLOCKS = ((0, 0, 4), (0, 4, 4), (0, 8, 4), (1, 0, 12), (2, 0, 12))
PIECES = ((0, 0, 4), (0, 4, 4), (0, 8, 4), (1, 0, 6), (1, 6, 6), (2, 0, 6), (2, 6, 6))
Y_FIRST = (1, 4, 5,)
ORDER = (
    (0,0), (0,1), (1,0,0,0,1), (1,0,0,-1,0), (0,2), (1,1,0,0,1), (1,0,1,0,0), (1,1,0,-1,0),
    (1,1,0,1,0), (1,2,0,0,1), (1,0,0,1,1), (1,0,1,0,1), (1,2,1,0,0), (1,2,0,-1,0), (1,1,0,1,1),
    (1,1,0,-1,1), (0,3), (1,0,1,-1,0), (1,2,0,1,1), (1,1,0,2,0), (1,2,1,0,1), (1,3,0,0,1),
    (1,4,0,0,1), (1,0,1,1,1), (1,2,1,-1,0), (1,1,0,2,1), (1,3,1,0,0), (0,4), (1,3,0,-1,0),
    (1,4,0,1,0), (1,5,0,0,1), (1,6,0,0,1), (1,4,0,-1,0), (1,3,1,0,1), (1,2,1,1,1), (1,3,0,1,1),
    (2,1), (1,4,0,1,1), (1,4,0,-1,1), (2,0), (1,6,1,0,0), (1,3,1,-1,0), (1,5,0,1,0),
    (1,5,0,-1,0), (1,6,0,-1,0), (1,6,1,0,1), (1,5,0,1,1), (1,6,0,1,1), (1,5,0,-1,1),
    (1,3,1,1,1), (2,2), (1,4,0,2,0), (1,4,0,2,1), (1,6,1,-1,0), (1,6,1,1,1), (1,5,0,2,0),
    (1,5,0,2,1), (2,4), (2,3), (2,6), (2,5),
)
CHUNKS = len(PIECES)

BF = jnp.bfloat16
F32 = jnp.float32


def kernel(
    gauge_h, energies_h, kmesh_h, lattice_h, degeneracy_h, path_h,
    out_l, out_p,
    gauge, energies, kmesh, lattice, degeneracy, path, in_s,
    at_ref, sc_ref, send, arrived, plain, other, gath, lmat, fpart, mixp, mixr,
    stage_l, stage_p, from_l, from_p, rows_f, rows_p, mix_f,
    a2a_s, a2a_r, g_s, g_r, f_s, f_r, m_s, m_r, o_s, o_r, op_s, op_r,
):
    loads = [
        pltpu.make_async_copy(src, dst, in_s.at[i])
        for i, (src, dst) in enumerate(
            (
                (energies_h, energies), (gauge_h, gauge), (kmesh_h, kmesh),
                (lattice_h, lattice), (degeneracy_h, degeneracy), (path_h, path),
            )
        )
    ]
    for load in loads:
        load.start()

    ka = lax.axis_index("ka")
    row = lax.axis_index("row")
    core = row % 2
    y = (row // 2) % 4
    zlo = row // 8
    x = ka // 4
    z = (ka % 4) * 2 + zlo
    turn = 2 * zlo - 1
    peers = [(dx, d) for d in (3, 2, 1, 0) for dx in (2, 1, 3, 0) if dx or d]

    def place_of(xx, zz):
        return (xx % 4) * 4 + zz // 2, (zz % 2) * 8 + row % 8
    mate = row + 1 - 2 * core

    def unit_of(z, yy, c):
        return z * 8 + yy * 2 + c

    yp = (y + 1) % 4
    ym = (y + 3) % 4
    yo = (y + 2) % 4
    zo = 1 - zlo

    barrier = pltpu.get_barrier_semaphore()
    for dx, d in peers:
        pl.semaphore_signal(
            barrier, inc=1, device_id=place_of(x + dx, (z + turn * d + 8) % 8),
            device_id_type=pl.DeviceIdType.MESH,
        )
    for i in range(1, NROW):
        pl.semaphore_signal(
            barrier, inc=1, device_id=(ka, (row + i) % NROW), device_id_type=pl.DeviceIdType.MESH
        )

    def remote(src, dst, ssem, rsem, dev):
        return pltpu.make_async_remote_copy(
            src_ref=src, dst_ref=dst, send_sem=ssem, recv_sem=rsem,
            device_id=dev, device_id_type=pl.DeviceIdType.MESH,
        )

    def wait_bytes(ref, sem):
        pltpu.make_async_copy(ref, ref, sem).wait()

    loads[0].wait()
    loads[1].wait()
    w = gauge.shape[1]
    e_col = jnp.transpose(jnp.broadcast_to(energies[...], (128, w)))
    e_full = jnp.concatenate([e_col] * (w // 128), 1)
    for p in range(2):
        u = gauge[p].astype(F32)
        at_ref[:, p * w : (p + 1) * w] = jnp.transpose(u).astype(BF)
        sc_ref[p] = (e_full * u).astype(BF)

    def rotate(cc):
        cols = slice(cc * 128, cc * 128 + 128)
        sr = sc_ref[0, :, cols]
        si = sc_ref[1, :, cols]
        rhs = jnp.concatenate(
            [jnp.concatenate([sr, si], 1), jnp.concatenate([si, -sr], 1)], 0
        )
        h = jnp.dot(at_ref[...], rhs, preferred_element_type=F32)
        for j in range(NKA):
            groups = [
                h[j * ROWS + t * 8 : j * ROWS + t * 8 + 8, p * 128 : p * 128 + 128]
                for t in range(ROWS // 8)
                for p in range(2)
            ]
            send[cc, j] = jnp.concatenate(groups, 0).astype(BF)

    def lines_of(i):
        return pl.ds(BLOCKS[i][1] * 4, BLOCKS[i][2] * 4)

    def spread(cc):
        for i, (tile, _, _) in enumerate(BLOCKS):
            if tile != cc:
                continue
            lines = lines_of(i)
            for dx, d in peers:
                to = place_of(x + dx, (z + turn * (0, 1, -2, 3)[d] + 8) % 8)
                remote(
                    send.at[cc, to[0], lines], arrived.at[cc, x * 4 + d, lines],
                    a2a_s.at[i], a2a_r.at[i], to,
                ).start()
        arrived[cc, pl.ds(x * 4, 1)] = send[cc, pl.ds(ka, 1)]

    rotate(0)
    pl.semaphore_wait(barrier, NKA - 1 + NROW - 1)
    spread(0)
    rotate(1)
    spread(1)
    rotate(2)
    spread(2)

    for load in loads[2:]:
        load.wait()
    nk = kmesh.shape[1]
    r_dev = lattice.shape[1]
    np_all = path.shape[1]

    def pad_rows(a):
        return jnp.concatenate([a.astype(F32), jnp.zeros((13, a.shape[1]), F32)], 0).astype(BF)

    lat = pad_rows(lattice[...])
    at_k = lax.broadcasted_iota(jnp.int32, (nk, nk), 0)
    pos = lax.broadcasted_iota(jnp.int32, (8, nk), 1)
    pos_z = pos >> 7
    from_z = ((ka % 4) * 2 + pos_z + (2 * pos_z - 1) * (pos & 3) + 8) & 7
    source = ((((pos >> 2) & 3) * 4 + (from_z >> 1)) * NROW) + (from_z & 1) * 8 + ((pos >> 4) & 7)
    order = jnp.where(at_k == source[:1], 1.0, 0.0).astype(BF)
    km = jnp.dot(pad_rows(kmesh[...]), order, preferred_element_type=F32).astype(BF)
    dims = (((0,), (0,)), ((), ()))
    wind = lax.dot_general(lat, km, dims, preferred_element_type=F32).astype(jnp.int32)
    wind = jnp.mod(wind + 23 * MESH, MESH)
    angle = wind.astype(F32) * (2.0 * math.pi / MESH)
    fcos = jnp.cos(angle).astype(BF)
    fsin = jnp.sin(angle).astype(BF)
    fpart[0, :, :nk] = fcos
    fpart[0, :, nk:] = fsin
    f_copy = remote(fpart.at[0], fpart.at[1], f_s, f_r, (ka, mate))
    f_copy.start()
    wind_p = lax.dot_general(pad_rows(path[...]), lat, dims, preferred_element_type=F32)
    wind_p = jnp.mod(wind_p.astype(jnp.int32) + 24 * PATH_DEN, PATH_DEN)
    angle_p = wind_p.astype(F32) * (2.0 * math.pi / PATH_DEN)
    weights = 1.0 / degeneracy[...].astype(F32)
    pcos = (jnp.cos(angle_p) * weights).astype(BF)
    psin = (jnp.sin(angle_p) * weights).astype(BF)
    pboth = jnp.concatenate([pcos, psin], 0)
    mc = jnp.dot(pboth, fcos, preferred_element_type=F32)
    ms = jnp.dot(pboth, fsin, preferred_element_type=F32)
    m_re = mc[:np_all] + ms[np_all:]
    m_im = mc[np_all:] - ms[:np_all]
    per_chip = np_all // (NROW // 2)
    for p in range(NROW // 2):
        mixp[p, :per_chip] = m_re[p * per_chip : (p + 1) * per_chip]
        mixp[p, per_chip:] = m_im[p * per_chip : (p + 1) * per_chip]
    for i in range(1, NROW):
        to = (row + i) % NROW
        remote(mixp.at[to // 2], mixr.at[row], m_s, m_r, (ka, to)).start()
    mixr[pl.ds(row, 1)] = mixp[pl.ds(row // 2, 1)]

    def take_block(i):
        cc, start, count = BLOCKS[i]
        lines = count * 4
        wait_bytes(arrived.at[cc, pl.ds(0, NKA - 1), lines_of(i)], a2a_r.at[i])
        block = arrived[cc, :, lines_of(i)]
        plain[: NKA * lines] = block.reshape(NKA * lines, 128).astype(F32)
        for g, (tile, first, rows) in enumerate(PIECES):
            if tile != cc or not start <= first < start + count:
                continue
            for half, dst in ((1 - core, other[g]), (core, gath[g].at[row])):
                for p in range(2):
                    for a in range(rows):
                        at = first + a - start
                        at = (at // 4) * 16 + p * 8 + at % 4 + half * 4
                        values = plain[pl.ds(at, NKA, stride=lines), :]
                        dst[p * rows + a] = values.astype(BF)
                if dst is other[g]:
                    remote(
                        other[g], gath[g].at[row], g_s.at[g], g_r.at[g, row], (ka, mate)
                    ).start()
            pass_on(g, 0, 0, 0)

    def unit_at(plane, dy, r):
        return unit_of((zlo + plane) % 2, (y + dy + 4) % 4, (core + r) % 2)

    def pass_on(g, plane, dy, r):
        u = unit_at(plane, dy, r)
        y_first = g in Y_FIRST
        to = []
        if plane == 0 or not y_first:
            if dy == 0 or (dy == -1 and r == 0):
                to.append(unit_of(zlo, yp, core))
            if dy == 0 or (dy == 1 and r == 1):
                to.append(unit_of(zlo, ym, core))
        if plane == 0 and (y_first or dy == 0):
            to.append(unit_of(zo, y, core))
        for t in to:
            remote(gath[g].at[u], gath[g].at[u], g_s.at[g], g_r.at[g, u], (ka, t)).start()

    def landed(g, plane, dy, r):
        u = unit_at(plane, dy, r)
        wait_bytes(gath[g].at[u], g_r.at[g, u])

    def build_factors():
        wait_bytes(mixr.at[pl.ds(0, NROW - 1)], m_r)
        f_copy.wait()
        for s in range(2):
            at = s * 2 * r_dev
            c_part = fpart[s, :, :nk]
            s_part = fpart[s, :, nk:]
            lmat[at : at + r_dev, :nk] = c_part
            lmat[at : at + r_dev, nk:] = s_part
            lmat[at + r_dev : at + 2 * r_dev, :nk] = -s_part
            lmat[at + r_dev : at + 2 * r_dev, nk:] = c_part
        total = mixr[0]
        for i in range(1, NROW):
            total = total + mixr[i]
        m_r4 = total[:per_chip]
        m_i4 = total[per_chip:]
        wide = jnp.concatenate(
            [jnp.concatenate([m_r4, -m_i4], 1), jnp.concatenate([m_i4, m_r4], 1)], 0
        )
        own_q = per_chip // 2
        for i in range(4):
            mix_f[i] = wide[i * own_q : (i + 1) * own_q]
        wide = jnp.concatenate([mix_f[2 * p + c] for c in (core, 1 - core) for p in range(2)], 0)
        high = wide.astype(BF)
        low = (wide - high.astype(F32)).astype(BF)
        lmat[4 * r_dev :, :] = jnp.concatenate([high.astype(F32), low.astype(F32)], 0).astype(BF)

    scale = 1.0 / nk

    def transform(g):
        cc, first, rows = PIECES[g]

        def one(i, carry):
            a = 2 * i
            re0 = gath[g][:, a].reshape(nk, 128)
            re1 = gath[g][:, a + 1].reshape(nk, 128)
            im0 = gath[g][:, rows + a].reshape(nk, 128)
            im1 = gath[g][:, rows + a + 1].reshape(nk, 128)
            both = jnp.concatenate(
                [jnp.concatenate([re0, re1], 1), jnp.concatenate([im0, im1], 1)], 0
            )
            product = jnp.dot(lmat[...], both, preferred_element_type=F32) * scale
            for b in range(2):
                v = product[:, b * 128 : b * 128 + 128]
                for p in range(2):
                    place(cc, p, core, first + a + b, v[p * r_dev : (p + 1) * r_dev])
                    stage_l[g][p, a + b] = v[(2 + p) * r_dev : (3 + p) * r_dev].astype(BF)
                vp = v[4 * r_dev : 4 * r_dev + 8] + v[4 * r_dev + 8 :]
                place_path(cc, core, first + a + b, vp[:4])
                stage_p[g][a + b] = vp
            return carry

        lax.fori_loop(0, rows // 2, one, 0)
        remote(stage_l[g], from_l[g], o_s.at[g], o_r.at[g], (ka, mate)).start()
        remote(stage_p[g], from_p[g], op_s.at[g], op_r.at[g], (ka, mate)).start()

    def row_at(half, a):
        return (a // 4) * 8 + half * 4 + a % 4

    def place(cc, p, half, a, value):
        rows_f[cc, p, pl.ds(row_at(half, a), r_dev, stride=ROWS), :] = value

    def place_path(cc, half, a, value):
        for p in range(2):
            rows_p[cc, p, pl.ds(row_at(half, a), 2, stride=ROWS), :] = value[2 * p : 2 * p + 2]

    def from_other_core(g):
        cc, first, rows = PIECES[g]
        wait_bytes(stage_l[g], o_r.at[g])
        wait_bytes(stage_p[g], op_r.at[g])

        def one(a, carry):
            for p in range(2):
                place(cc, p, 1 - core, first + a, from_l[g][p, a].astype(F32))
            place_path(cc, 1 - core, first + a, from_p[g][a, 4:])
            return carry

        lax.fori_loop(0, rows, one, 0)

    def write_out(cc):
        step = 8

        def one(i, carry):
            at = pl.multiple_of(i * step * ROWS, step * ROWS)
            for p in range(2):
                cols = slice((p * TILES + cc) * 128, (p * TILES + cc + 1) * 128)
                block = rows_f[cc, p, pl.ds(at, step * ROWS), :].astype(BF)
                out_l[pl.ds(i * step, step), :, cols] = block.reshape(step, ROWS, 128)
            return carry

        lax.fori_loop(0, r_dev // step, one, 0)
        for p in range(2):
            cols = slice((p * TILES + cc) * 128, (p * TILES + cc + 1) * 128)
            for q in range(2):
                out_p[q, :, cols] = rows_p[cc, p, q * ROWS : (q + 1) * ROWS, :]

    everything = [(pn, dy, r) for pn in range(2) for dy in (0, -1, 1, 2) for r in range(2)][1:]
    pending = {g: list(everything) for g in range(CHUNKS)}
    left = {cc: sum(t == cc for t, _, _ in PIECES) for cc in range(TILES)}

    def finish(g):
        from_other_core(g)
        left[PIECES[g][0]] -= 1
        if left[PIECES[g][0]] == 0:
            write_out(PIECES[g][0])

    last = None
    for what, g, *unit in ORDER:
        if what == 0:
            take_block(g)
        elif what == 1:
            landed(g, *unit)
            pending[g].remove(tuple(unit))
            pass_on(g, *unit)
        else:
            if last is None:
                build_factors()
            for rest in pending[g]:
                landed(g, *rest)
            transform(g)
            if last is not None:
                finish(last)
            last = g
    finish(last)

    for i, (cc, _, _) in enumerate(BLOCKS):
        wait_bytes(send.at[cc, pl.ds(0, NKA - 1), lines_of(i)], a2a_s.at[i])
    wait_bytes(mixr.at[pl.ds(0, NROW - 1)], m_s)
    for g in range(CHUNKS):
        wait_bytes(gath[g].at[pl.ds(0, NROW - 1)], g_s.at[g])
        wait_bytes(stage_l[g], o_s.at[g])
        wait_bytes(stage_p[g], op_s.at[g])


def local(gauge, energies, kmesh, lattice, degeneracy, path):
    w = gauge.shape[2]
    nk = kmesh.shape[1]
    r_dev = lattice.shape[1]
    path_dev = path.shape[1] // NROW
    vmem = pl.BlockSpec(memory_space=pltpu.VMEM)
    dma = pltpu.SemaphoreType.DMA
    hbm = pl.BlockSpec(memory_space=pltpu.HBM)
    rows = [n for _, _, n in PIECES]
    return pl.pallas_call(
        kernel,
        out_shape=(
            jax.ShapeDtypeStruct((r_dev, ROWS, 2 * w), BF),
            jax.ShapeDtypeStruct((path_dev, ROWS, 2 * w), F32),
        ),
        in_specs=[hbm] * 6,
        out_specs=(vmem, vmem),
        scratch_shapes=[
            pltpu.VMEM((2, w, w), BF),
            pltpu.VMEM((1, w), F32),
            pltpu.VMEM((3, nk), jnp.int32),
            pltpu.VMEM((3, r_dev), jnp.int32),
            pltpu.VMEM((1, r_dev), jnp.int32),
            pltpu.VMEM(path.shape, jnp.int32),
            dma((6,)),
            pltpu.VMEM((w, 2 * w), BF),
            pltpu.VMEM((2, w, w), BF),
            pltpu.VMEM((TILES, NKA, 2 * ROWS, 128), BF),
            pltpu.VMEM((TILES, NKA, 2 * ROWS, 128), BF),
            pltpu.VMEM(((NKA + 1) * 2 * ROWS, 128), F32),
            [pltpu.VMEM((2 * n, NKA, 128), BF) for n in rows],
            [pltpu.VMEM((NROW, 2 * n, NKA, 128), BF) for n in rows],
            pltpu.VMEM((4 * r_dev + 16, 2 * nk), BF),
            pltpu.VMEM((2, r_dev, 2 * nk), BF),
            pltpu.VMEM((NROW // 2, 8, nk), F32),
            pltpu.VMEM((NROW, 8, nk), F32),
            [pltpu.VMEM((2, n, r_dev, 128), BF) for n in rows],
            [pltpu.VMEM((n, 8, 128), F32) for n in rows],
            [pltpu.VMEM((2, n, r_dev, 128), BF) for n in rows],
            [pltpu.VMEM((n, 8, 128), F32) for n in rows],
            pltpu.VMEM((TILES, 2, (r_dev + 1) * ROWS, 128), F32),
            pltpu.VMEM((TILES, 2, (path_dev + 1) * ROWS, 128), F32),
            pltpu.VMEM((4, path_dev, 2 * nk), F32),
            dma((len(BLOCKS),)),
            dma((len(BLOCKS),)),
            dma((CHUNKS,)),
            dma((CHUNKS, NROW)),
            dma,
            dma,
            dma,
            dma,
            dma((CHUNKS,)),
            dma((CHUNKS,)),
            dma((CHUNKS,)),
            dma((CHUNKS,)),
        ],
        compiler_params=pltpu.CompilerParams(
            collective_id=0, has_side_effects=True, vmem_limit_bytes=48 << 20
        ),
    )(
        *[
            pltpu.with_memory_space_constraint(v, pltpu.HBM)
            for v in (gauge[0], energies, kmesh, lattice, degeneracy[None, :], path)
        ]
    )


def solution(mesh):
    return jax.shard_map(
        local,
        mesh=mesh,
        in_specs=(
            P(("ka", "row"), None, None, None),
            P(("ka", "row"), None),
            P(),
            P(None, "row"),
            P("row"),
            P(),
        ),
        out_specs=(P("row", "ka", None), P("row", "ka", None)),
        check_vma=False,
    )
```
